32 devices in a mesh: gx: 8 (over z, x), gy: 2 (over core), gz: 2 (over y).
Axes of the slice: x: 2, y: 2, z: 4, core: 2. Of those that a mesh axis runs over, the one named last changes fastest.
Arguments:
- feats: bfloat16 [8, 2, 2, 128, 256], P('gx', 'gy', 'gz'), may hold values from -6 to 6
- positions: float32 [8, 2, 2, 3, 128], P('gx', 'gy', 'gz'), may hold values from 0 to 1
- species: int32 [8, 2, 2, 128], P('gx', 'gy', 'gz'), may hold values from 0 to 5
- cell_counts: int32 [8, 2, 2], P('gx', 'gy', 'gz'), may hold values from 16 to 128, as said below
- pair_list: int32 [8, 2, 2, 27], P('gx', 'gy', 'gz'), may hold values 0 or 1
- w_env: bfloat16 [256, 64], replicated, may hold values from -0.375 to 0.375
- radial: float32 [4, 64], replicated, may hold values from -3 to 3
- pair_scale: float32 [6, 6], replicated, may hold values from 0.5 to 2
- w_hidden: bfloat16 [256, 256], replicated, may hold values from -0.375 to 0.375
- w_zero: bfloat16 [64, 256], replicated, may hold values from -0.75 to 0.75
- w_one: bfloat16 [64, 256], replicated, may hold values from -0.25 to 0.25
- w_out: float32 [256], replicated, may hold values from -0.375 to 0.375
Outputs:
- atom_energy: float32 [8, 2, 2, 128], P('gx', 'gy', 'gz')
- forces: float32 [8, 2, 2, 3, 128], P('gx', 'gy', 'gz')
- feat_grad: bfloat16 [8, 2, 2, 128, 256], P('gx', 'gy', 'gz')
The draws below stay inside these ranges and needn't reach their ends.
Inputs may be any that keep to these rules, and one draw needn't show every extreme that they name: `cell_counts`: slots at or beyond a cell's count are empty and carry no atom.
All inputs are finite; a program needn't handle non-finite values. No bound on the sum of `pair_list` on one device may be relied on, other than what follows from the above.
Results may differ from the reference program's by a relative error of at most 0.0066.
Values may be sent and summed in bfloat16 or wider, within the bound.
No kernel may reach another device: no remote copies, remote signals or barrier semaphores. Data moves between devices by JAX's collectives and lax.ppermute only.
A program may use at most 64 MiB of HBM per device.

```python
import math
import jax
import jax.numpy as jnp
import numpy as np
from jax import lax

D = 256
CHANNELS = 64
NBASIS = 4
NSPEC = 6
SLOTS = 128
NCX = 8
NCY = 2
NCZ = 2


def draw_cell_counts(key, part):
    key_floor, key_fill, key_top, key_low = jax.random.split(jax.random.fold_in(key, 11), 4)
    total_cells = NCX * NCY * NCZ
    floor_level = jax.random.randint(key_floor, (NCX, 1, 1), SLOTS // 8, SLOTS * 3 // 4 + 1)
    raw_fill = jax.random.randint(key_fill, (NCX, NCY, NCZ), 0, 1 << 20)
    counted = floor_level + raw_fill % (SLOTS + 1 - floor_level)
    flat_counts = counted.reshape(total_cells)
    top_spot = jax.random.randint(key_top, (), 0, total_cells)
    low_spot = (top_spot + 1 + jax.random.randint(key_low, (), 0, total_cells - 1)) % total_cells
    flat_counts = flat_counts.at[top_spot].set(SLOTS).at[low_spot].set(SLOTS // 8)
    return flat_counts.reshape(NCX, NCY, NCZ).astype(jnp.int32)


def plant(values, own_key, low, top_value):
    dims = values.shape
    index_at = [jax.random.randint(jax.random.fold_in(own_key, axis), (), 0, dims[axis]) for axis in range(len(dims))]
    values = values.at[tuple(index_at)].set(low)
    longest = dims.index(max(dims))
    index_at[longest] = (index_at[longest] + 1) % dims[longest]
    return values.at[tuple(index_at)].set(top_value)


def block_levels(rng, extent, cuts, smallest, high):
    factor_of, own = 1.0, jax.random.fold_in(rng, 6)
    for position, parts in cuts:
        heights = jnp.exp(jax.random.uniform(jax.random.fold_in(own, position), (parts,), jnp.float32, smallest / len(cuts), high / len(cuts)))
        factor_of = factor_of * jnp.repeat(heights, extent[position] // parts).reshape([-1 if axis == position else 1 for axis in range(len(extent))])
    return factor_of


def gaussian(stream_key, extent, width, reach, pieces=(), kind=jnp.bfloat16):
    loudness = block_levels(stream_key, extent, pieces, -0.22, 0.18) if pieces else 1.0
    result = jax.random.normal(stream_key, extent, jnp.float32) * width * loudness
    return jnp.minimum(jnp.maximum(result, -reach), reach).astype(kind)


def setup_inputs(seed: int = 0) -> dict:
    key_of = jax.random.split(jax.random.key(seed), 13)
    feats = gaussian(key_of[0], (NCX, NCY, NCZ, SLOTS, D), 1.0, 6.0, ((0, 8), (1, 2), (2, 2)))
    positions = jnp.clip(1.0 * jax.random.uniform(key_of[1], (NCX, NCY, NCZ, 3, SLOTS), jnp.float32) ** block_levels(key_of[1], (NCX, NCY, NCZ, 3, SLOTS), ((0, 8), (1, 2), (2, 2)), -0.2, 0.2), 0.0, 1.0)
    species = plant(jax.random.randint(key_of[2], (NCX, NCY, NCZ, SLOTS), 0, NSPEC), jax.random.fold_in(key_of[2], 1), 0, NSPEC - 1).astype(jnp.int32)
    cell_counts = draw_cell_counts(jax.random.fold_in(key_of[12], 71), 0)
    pair_list = plant((jax.random.randint(key_of[4], (NCX, NCY, NCZ, 27), 0, 3) < 2).astype(jnp.int32), jax.random.fold_in(key_of[4], 1), 0, 1)
    w_env = gaussian(key_of[5], (D, CHANNELS), D ** -0.5, 0.375)
    radial = gaussian(key_of[6], (NBASIS, CHANNELS), 0.5, 3.0, (), jnp.float32)
    pair_scale = jnp.clip(jnp.exp(jax.random.uniform(key_of[7], (NSPEC, NSPEC), jnp.float32, math.log(0.5), math.log(2.0))), 0.5, 2.0)
    w_hidden = gaussian(key_of[8], (D, D), D ** -0.5, 0.375)
    w_zero = gaussian(key_of[9], (CHANNELS, D), CHANNELS ** -0.5, 0.75)
    w_one = gaussian(key_of[10], (CHANNELS, D), (8 * CHANNELS) ** -0.5, 0.25)
    w_out = gaussian(key_of[11], (D,), D ** -0.5, 0.375, (), jnp.float32)
    return dict(feats=feats, positions=positions, species=species, cell_counts=cell_counts, pair_list=pair_list, w_env=w_env, radial=radial, pair_scale=pair_scale, w_hidden=w_hidden, w_zero=w_zero, w_one=w_one, w_out=w_out)


CUTOFF = 0.55

def neighbour_table(size_x, size_y, size_z):
    cell_ids = np.arange(size_x * size_y * size_z)
    cell_x = cell_ids // (size_y * size_z)
    cell_y = cell_ids // size_z % size_y
    cell_z = cell_ids % size_z
    columns = []
    for offset_index in range(27):
        step_x = offset_index // 9 - 1
        step_y = offset_index // 3 % 3 - 1
        step_z = offset_index % 3 - 1
        columns.append((cell_x + step_x) % size_x * size_y * size_z + (cell_y + step_y) % size_y * size_z + (cell_z + step_z) % size_z)
    return np.stack(columns, axis=1).astype(np.int32)

def pair_terms(pos_i, pos_j, offset_index):
    offset = jnp.stack([offset_index // 9 - 1, offset_index // 3 % 3 - 1, offset_index % 3 - 1]).astype(jnp.float32)
    relative = offset[:, None, None] + pos_j[:, None, :] - pos_i[:, :, None]
    scaled = lax.optimization_barrier(jnp.sum(relative * relative, axis=0)) / (CUTOFF * CUTOFF)
    inside = jnp.maximum(1.0 - scaled, 0.0)
    envelope = inside * inside
    centers = (jnp.arange(NBASIS, dtype=jnp.float32) + 0.5) / NBASIS
    spread = (scaled[None] - centers[:, None, None]) * NBASIS
    radial_basis = jnp.exp(-spread * spread)
    harmonic = jnp.concatenate([jnp.ones_like(scaled)[None], relative / CUTOFF], axis=0)
    return (relative, scaled, inside, envelope, spread, radial_basis, harmonic)

def tile_weight(onehot_i, occupied_i, coef_j, listed, offset_index):
    species_pair = jnp.dot(onehot_i.T, coef_j, precision=lax.Precision.HIGHEST, preferred_element_type=jnp.float32)
    self_tile = (offset_index == 13).astype(jnp.float32)
    not_self = 1.0 - self_tile * jnp.eye(SLOTS, dtype=jnp.float32)
    return species_pair * not_self * occupied_i[:, None] * listed

def build_tile(weight, envelope, radial_basis, harmonic):
    full = (weight * envelope)[None, None] * radial_basis[:, None] * harmonic[None, :]
    return full.astype(jnp.bfloat16).reshape(4 * NBASIS * SLOTS, SLOTS)

def pair_grad(tile_grad, terms, weight):
    relative, scaled, inside, envelope, spread, radial_basis, harmonic = terms
    through_basis = lax.optimization_barrier(jnp.sum(tile_grad * harmonic[None], axis=1))
    value_part = lax.optimization_barrier(jnp.sum(through_basis * radial_basis, axis=0))
    slope_part = lax.optimization_barrier(jnp.sum(through_basis * radial_basis * spread, axis=0)) * (-2.0 * NBASIS)
    vector_part = lax.optimization_barrier(jnp.sum(tile_grad[:, 1:] * radial_basis[:, None], axis=0))
    grad_scaled = weight * (-2.0 * inside * value_part + envelope * slope_part)
    return grad_scaled[None] * (2.0 / (CUTOFF * CUTOFF)) * relative + (weight * envelope)[None] * vector_part / CUTOFF

def reference(feats, positions, species, cell_counts, pair_list, w_env, radial, pair_scale, w_hidden, w_zero, w_one, w_out):
    cell_total = NCX * NCY * NCZ
    feat_rows = feats.reshape(cell_total * SLOTS, D)
    pos_rows = positions.reshape(cell_total, 3, SLOTS)
    slot_ids = jnp.arange(SLOTS, dtype=jnp.int32)
    occupied = (slot_ids[None, :] < cell_counts.reshape(cell_total, 1)).astype(jnp.float32)
    onehot = (species.reshape(cell_total, 1, SLOTS) == jnp.arange(NSPEC, dtype=jnp.int32)[None, :, None]).astype(jnp.float32)
    species_coef = jnp.einsum('st,ctj->csj', pair_scale, onehot, precision=lax.Precision.HIGHEST) * occupied[:, None, :]
    chans = jnp.dot(feat_rows, w_env, preferred_element_type=jnp.float32).astype(jnp.bfloat16).reshape(cell_total, SLOTS, CHANNELS)
    neighbours = jnp.asarray(neighbour_table(NCX, NCY, NCZ))
    listed_all = pair_list.reshape(cell_total, 27).astype(jnp.float32)

    def tile_setup(own_cell, offset_index):
        neighbour = neighbours[own_cell, offset_index]
        weight = tile_weight(onehot[own_cell], occupied[own_cell], species_coef[neighbour], listed_all[own_cell, offset_index], offset_index)
        terms = pair_terms(pos_rows[own_cell], pos_rows[neighbour], offset_index)
        pair_tile = build_tile(weight, terms[3], terms[5], terms[6])
        return (neighbour, weight, terms, pair_tile)

    def forward_cell(own_cell):

        def add_tile(offset_index, running):
            neighbour, weight, terms, pair_tile = tile_setup(own_cell, offset_index)
            return running + jnp.dot(pair_tile, chans[neighbour], preferred_element_type=jnp.float32)
        moments = lax.fori_loop(0, 27, add_tile, jnp.zeros((4 * NBASIS * SLOTS, CHANNELS), jnp.float32))
        return jnp.einsum('kc,kmic->mic', radial, moments.reshape(NBASIS, 4, SLOTS, CHANNELS), precision=lax.Precision.HIGHEST)
    vectors = lax.map(forward_cell, jnp.arange(cell_total, dtype=jnp.int32))
    scalar_zero = vectors[:, 0].reshape(cell_total * SLOTS, CHANNELS).astype(jnp.bfloat16)
    scalar_one = lax.optimization_barrier(jnp.sum(vectors[:, 1:] * vectors[:, 1:], axis=1)).reshape(cell_total * SLOTS, CHANNELS).astype(jnp.bfloat16)
    pre = jnp.dot(feat_rows, w_hidden, preferred_element_type=jnp.float32)
    pre = pre + jnp.dot(scalar_zero, w_zero, preferred_element_type=jnp.float32)
    pre = pre + jnp.dot(scalar_one, w_one, preferred_element_type=jnp.float32)
    gate = jax.nn.sigmoid(pre)
    occupied_rows = occupied.reshape(cell_total * SLOTS, 1)
    atom_energy = occupied.reshape(cell_total * SLOTS) * jnp.dot(pre * gate, w_out, precision=lax.Precision.HIGHEST)
    pre_grad = (occupied_rows * w_out[None, :] * gate * (1.0 + pre * (1.0 - gate))).astype(jnp.bfloat16)
    direct_grad = jnp.dot(pre_grad, w_hidden.T, preferred_element_type=jnp.float32)
    zero_grad = jnp.dot(pre_grad, w_zero.T, preferred_element_type=jnp.float32).reshape(cell_total, SLOTS, CHANNELS)
    one_grad = jnp.dot(pre_grad, w_one.T, preferred_element_type=jnp.float32).reshape(cell_total, SLOTS, CHANNELS)
    vector_grad = jnp.concatenate([zero_grad[:, None], 2.0 * vectors[:, 1:] * one_grad[:, None]], axis=1)

    def backward_cell(accum, own_cell):
        moment_grad = (radial[:, None, None, :] * vector_grad[own_cell][None]).astype(jnp.bfloat16).reshape(4 * NBASIS * SLOTS, CHANNELS)

        def back_tile(offset_index, partial_sums):
            chan_grad, pos_grad = partial_sums
            neighbour, weight, terms, pair_tile = tile_setup(own_cell, offset_index)
            to_chans = lax.dot_general(pair_tile, moment_grad, (((0,), (0,)), ((), ())), preferred_element_type=jnp.float32)
            tile_grad = jnp.dot(moment_grad, chans[neighbour].T, preferred_element_type=jnp.float32).reshape(NBASIS, 4, SLOTS, SLOTS)
            rel_grad = pair_grad(tile_grad, terms, weight)
            chan_grad = chan_grad.at[neighbour].add(to_chans)
            pos_grad = pos_grad.at[neighbour].add(lax.optimization_barrier(jnp.sum(rel_grad, axis=1)))
            pos_grad = pos_grad.at[own_cell].add(-lax.optimization_barrier(jnp.sum(rel_grad, axis=2)))
            return (chan_grad, pos_grad)
        return (lax.fori_loop(0, 27, back_tile, accum), None)
    initial = (jnp.zeros((cell_total, SLOTS, CHANNELS), jnp.float32), jnp.zeros((cell_total, 3, SLOTS), jnp.float32))
    sums_out, unused = lax.scan(backward_cell, initial, jnp.arange(cell_total, dtype=jnp.int32))
    chan_grad, pos_grad = sums_out
    feat_grad = direct_grad + jnp.dot(chan_grad.reshape(cell_total * SLOTS, CHANNELS), w_env.astype(jnp.float32).T, precision=lax.Precision.HIGHEST)
    return (atom_energy.reshape(NCX, NCY, NCZ, SLOTS), (-pos_grad).reshape(NCX, NCY, NCZ, 3, SLOTS), feat_grad.astype(jnp.bfloat16).reshape(NCX, NCY, NCZ, SLOTS, D))
```

```python
import jax
import jax.numpy as jnp
from jax import lax
from jax.experimental import pallas as pl
from jax.experimental.pallas import tpu as pltpu
from jax.sharding import PartitionSpec as P

D = 256
CHANNELS = 64
NBASIS = 4
NSPEC = 6
SLOTS = 128
CUTOFF = 0.55
CENTRE = 0.5
ROWS = 80
POS_ROW = 64
CODE_ROW = 73
OFFSETS = 27
CHUNK = 16
CHUNKS = SLOTS // CHUNK
QUAD = NBASIS * SLOTS
WIDE = 4 * CHANNELS
LANES = 2 * SLOTS
PAIRS = (OFFSETS + 1) // 2
F32 = jnp.float32
BF16 = jnp.bfloat16


def dot_nn(a, b):
    return lax.dot_general(a, b, (((1,), (0,)), ((), ())), preferred_element_type=F32)


def dot_nt(a, b):
    return lax.dot_general(a, b, (((1,), (1,)), ((), ())), preferred_element_type=F32)


def split3(value):
    high = value.astype(BF16)
    rest = value - high.astype(F32)
    middle = rest.astype(BF16)
    low = (rest - middle.astype(F32)).astype(BF16)
    return high, middle, low


def pack_kernel(counts_ref, feats_ref, pos_ref, species_ref, w_env_ref, msg_ref):
    chans = lax.dot_general(
        w_env_ref[...],
        feats_ref[0, 0, 0],
        (((0,), (1,)), ((), ())),
        preferred_element_type=F32,
    )
    msg_ref[0, :CHANNELS] = chans.astype(BF16)
    pos = pos_ref[0, 0, 0]
    slots = lax.broadcasted_iota(jnp.int32, (1, SLOTS), 1)
    code = jnp.where(slots < counts_ref[0, 0, 0], species_ref[0, 0].astype(F32), -1.0)
    high = pos.astype(BF16).astype(F32)
    middle = (pos - high).astype(BF16).astype(F32)
    low = pos - high - middle
    tail = jnp.concatenate([high, middle, low, code, jnp.zeros((6, SLOTS), F32)], axis=0)
    msg_ref[0, CHANNELS:] = tail.astype(BF16)


def unique_of(offset, count):
    if count == 2:
        return jnp.where(offset == 0, 0, 1)
    return jnp.where(offset == 0, 0, jnp.where(offset > 0, 1, 2))


def main_kernel(shape, *refs):
    nxu, nyu, nzu, sizes = shape
    cells = nxu * nyu * nzu
    refs = list(refs)
    list_ref = refs.pop(0)
    msg_refs = [refs.pop(0) for _ in range(nxu)]
    (feats_ref, radial_ref, scale_ref, w_hidden_ref, w_zero_ref, w_one_ref, w_out_ref) = refs[:7]
    refs = refs[7:]
    energy_ref, direct_ref = refs[:2]
    out_refs = refs[2 : 2 + nyu]
    (
        order, xi, weight, xj, chan, tiles, rmat, s_all, r_all, wb_all,
        acc, pbuf, grad, gradt, fi, cg, pg,
    ) = refs[2 + nyu :]

    def count_listed(index, found):
        order[found] = index
        return found + list_ref[0, 0, 0, index]

    live = lax.fori_loop(0, OFFSETS, count_listed, jnp.int32(0))
    order[live] = jnp.int32(OFFSETS)
    trips = (live + 1) // 2

    code_rows = []
    for cell in range(cells):
        msg = msg_refs[cell // (nyu * nzu)]
        at = cell % (nyu * nzu)
        tail = msg[at, CHANNELS:].astype(F32)
        place = tail[0:3] + tail[3:6] + tail[6:9]
        xj[cell, 0:3] = (place - CENTRE) * (1.0 / CUTOFF)
        code_rows.append(tail[9:10])
        chan[cell] = msg[at, :CHANNELS]
        cg[cell] = jnp.zeros((CHANNELS, SLOTS), F32)
        pg[cell] = jnp.zeros((8, SLOTS), F32)
    for axis in range(3):
        row = jnp.broadcast_to(xj[0, axis : axis + 1], (SLOTS, SLOTS))
        xi[axis] = row.T
    code_i = jnp.broadcast_to(code_rows[0], (SLOTS, SLOTS)).T
    lane = lax.broadcasted_iota(jnp.int32, (SLOTS, SLOTS), 1)
    sub = lax.broadcasted_iota(jnp.int32, (SLOTS, SLOTS), 0)
    onehot = jnp.where((code_i == (lane % 8).astype(F32)) & (lane < 24), 1.0, 0.0)
    onehot = onehot.astype(BF16)
    scale = scale_ref[...]
    coef = []
    for cell in range(cells):
        total = jnp.zeros((8, SLOTS), F32)
        for kind in range(NSPEC):
            column = jnp.broadcast_to(scale[:, kind : kind + 1], (8, SLOTS))
            total = total + jnp.where(code_rows[cell] == float(kind), column, 0.0)
        high = total.astype(BF16).astype(F32)
        middle = (total - high).astype(BF16).astype(F32)
        low = total - high - middle
        coef.append(
            jnp.concatenate([high, middle, low, jnp.zeros((104, SLOTS), F32)], axis=0).astype(BF16)
        )
    for cell in range(cells):
        strength = dot_nn(onehot, coef[cell])
        if cell == 0:
            strength = jnp.where(lane == sub, 0.0, strength)
        weight[cell] = strength
    weight[cells] = jnp.zeros((SLOTS, SLOTS), F32)
    acc[...] = jnp.zeros_like(acc)
    fi[...] = jnp.zeros_like(fi)

    def place_of(tile):
        real = tile < OFFSETS
        held = jnp.where(real, tile, 13)
        ox = held // 9 - 1
        oy = held // 3 % 3 - 1
        oz = held % 3 - 1
        ux = unique_of(ox, sizes[0])
        uy = unique_of(oy, sizes[1])
        uz = unique_of(oz, sizes[2])
        cell = (ux * nzu + uz) * nyu + uy
        shifts = [o.astype(F32) * (1.0 / CUTOFF) for o in (ox, oy, oz)]
        return cell, jnp.where(real, cell, cells), shifts

    def rows_of(pair):
        first, second = order[2 * pair], order[2 * pair + 1]
        cell_a, weight_a, shift_a = place_of(first)
        cell_b, weight_b, shift_b = place_of(second)
        rows = [
            jnp.concatenate(
                [
                    xj[cell_a, axis : axis + 1] + shift_a[axis],
                    xj[cell_b, axis : axis + 1] + shift_b[axis],
                ],
                axis=1,
            )
            for axis in range(3)
        ]
        return cell_a, cell_b, weight_a, weight_b, rows

    def relative(rows, block):
        out = []
        for axis in range(3):
            own = xi[axis, block * CHUNK : (block + 1) * CHUNK]
            out.append(rows[axis] - jnp.concatenate([own, own], axis=1))
        return out

    def forward(pair, carry):
        cell_a, cell_b, weight_a, weight_b, rows = rows_of(pair)
        values = jnp.concatenate([chan[cell_a], chan[cell_b]], axis=1)
        rmat[pair, :CHANNELS] = values
        wide = values.astype(F32)
        for axis in range(3):
            base = (axis + 1) * CHANNELS
            rmat[pair, base : base + CHANNELS] = (wide * rows[axis]).astype(BF16)
        for block in range(CHUNKS):
            at = slice(block * CHUNK, (block + 1) * CHUNK)
            dx, dy, dz = relative(rows, block)
            s = jnp.minimum(dx * dx + dy * dy + dz * dz, 1.0)
            inside = 1.0 - s
            spread = 4.0 * s - 0.5
            ratio = jnp.exp(8.0 * s)
            strength = jnp.concatenate([weight[weight_a, at], weight[weight_b, at]], axis=1)
            wb = strength * jnp.exp(-(spread * spread))
            s_all[pair, at] = s
            r_all[pair, at] = ratio
            wb_all[pair, at] = wb
            tile = wb * (inside * inside)
            for k in range(NBASIS):
                base = block * 4 * CHUNK + k * CHUNK
                tiles[pair, base : base + CHUNK] = tile.astype(BF16)
                if k + 1 < NBASIS:
                    tile = tile * ratio
        acc[...] += dot_nt(tiles[pair], rmat[pair])
        return carry

    lax.fori_loop(0, trips, forward, 0)

    radial = radial_ref[...]
    weights_k = []
    for k in range(NBASIS):
        row = radial[k : k + 1] * LADDER[k]
        weights_k.append(jnp.concatenate([row] * 4, axis=1))
    mixed = []
    for block in range(CHUNKS):
        base = block * 4 * CHUNK
        total = weights_k[0] * acc[base : base + CHUNK]
        for k in range(1, NBASIS):
            total = total + weights_k[k] * acc[base + k * CHUNK : base + (k + 1) * CHUNK]
        mixed.append(total)
    mixed = jnp.concatenate(mixed, axis=0)
    scalar = mixed[:, :CHANNELS]
    vectors = [
        mixed[:, (axis + 1) * CHANNELS : (axis + 2) * CHANNELS] - xi[axis][:, :CHANNELS] * scalar
        for axis in range(3)
    ]
    norms = vectors[0] * vectors[0] + vectors[1] * vectors[1] + vectors[2] * vectors[2]
    pre = dot_nn(feats_ref[0, 0, 0], w_hidden_ref[...])
    pre = pre + dot_nn(scalar.astype(BF16), w_zero_ref[...])
    pre = pre + dot_nn(norms.astype(BF16), w_one_ref[...])
    gate = jax.nn.sigmoid(pre)
    w_out = w_out_ref[...]
    occupied = code_i >= 0.0
    energy = jnp.sum(pre * gate * w_out, axis=1, keepdims=True)
    energy = jnp.where(occupied, jnp.broadcast_to(energy, (SLOTS, SLOTS)), 0.0).T
    energy_ref[0, 0] = energy[0:1]
    occupied_wide = jnp.concatenate([occupied, occupied], axis=1)
    pre_grad = jnp.where(occupied_wide, w_out * gate * (1.0 + pre * (1.0 - gate)), 0.0)
    pre_grad = pre_grad.astype(BF16)
    direct_ref[...] = dot_nt(pre_grad, w_hidden_ref[...])
    zero_grad = dot_nt(pre_grad, w_zero_ref[...])
    one_grad = 2.0 * dot_nt(pre_grad, w_one_ref[...])
    parts = [vector * one_grad for vector in vectors]
    own_force = [jnp.sum(part * scalar, axis=1, keepdims=True) for part in parts]
    head = zero_grad
    for axis in range(3):
        head = head - xi[axis][:, :CHANNELS] * parts[axis]
    full = jnp.concatenate([head] + parts, axis=1)
    for block in range(CHUNKS):
        piece = full[block * CHUNK : (block + 1) * CHUNK]
        for k in range(NBASIS):
            base = block * 4 * CHUNK + k * CHUNK
            scaled = weights_k[k] * piece
            grad[base : base + CHUNK] = scaled.astype(BF16)
            pbuf[base : base + CHUNK] = scaled
    for step in range(QUAD // SLOTS):
        for half in range(WIDE // SLOTS):
            lanes = slice(half * SLOTS, (half + 1) * SLOTS)
            rows = slice(step * SLOTS, (step + 1) * SLOTS)
            gradt[lanes, rows] = pbuf[rows, lanes].T.astype(BF16)

    def backward(pair, carry):
        cell_a, cell_b, weight_a, weight_b, rows = rows_of(pair)
        pbuf[...] = dot_nn(grad[...], rmat[pair])
        back = dot_nn(gradt[...], tiles[pair])
        values = rmat[pair, :CHANNELS].astype(F32)
        sums = back[:CHANNELS]
        along = []
        for axis in range(3):
            part = back[(axis + 1) * CHANNELS : (axis + 2) * CHANNELS]
            sums = sums + rows[axis] * part
            along.append(jnp.sum(values * part, axis=0, keepdims=True))
        cg[cell_a] += sums[:, :SLOTS]
        cg[cell_b] += sums[:, SLOTS:]
        totals = [jnp.zeros((CHUNK, LANES), F32) for _ in range(3)]
        for block in range(CHUNKS):
            at = slice(block * CHUNK, (block + 1) * CHUNK)
            s = s_all[pair, at]
            ratio = r_all[pair, at]
            inside = 1.0 - s
            step = 8.0 * inside
            level = -2.0 - step * (4.0 * s - 0.5)
            levels = [level]
            for k in range(1, NBASIS):
                levels.append(levels[-1] + step)
            base = block * 4 * CHUNK
            slope = levels[3] * pbuf[base + 3 * CHUNK : base + 4 * CHUNK]
            for k in (2, 1, 0):
                slope = slope * ratio + levels[k] * pbuf[base + k * CHUNK : base + (k + 1) * CHUNK]
            slope = slope * (wb_all[pair, at] * inside)
            for axis, delta in enumerate(relative(rows, block)):
                push = slope * delta
                totals[axis] = totals[axis] + push
                fi[axis, at] += push[:, :SLOTS] + push[:, SLOTS:]
        for axis in range(3):
            total = jnp.sum(totals[axis], axis=0, keepdims=True) * 2.0 + along[axis]
            pg[cell_a, axis : axis + 1] += total[:, :SLOTS]
            pg[cell_b, axis : axis + 1] += total[:, SLOTS:]
        return carry

    lax.fori_loop(0, trips, backward, 0)

    for axis in range(3):
        column = jnp.sum(fi[axis], axis=1, keepdims=True) * 2.0 + own_force[axis]
        row = jnp.broadcast_to(column, (SLOTS, SLOTS)).T
        pg[0, axis : axis + 1] -= row[0:1]
    for uy in range(nyu):
        for uz in range(nzu):
            for ux in range(nxu):
                cell = (ux * nzu + uz) * nyu + uy
                kind = out_refs[uy].dtype
                at = uz * nxu + ux
                out_refs[uy][at, :CHANNELS] = cg[cell].astype(kind)
                tail = jnp.concatenate([pg[cell], jnp.zeros((8, SLOTS), F32)], axis=0)
                out_refs[uy][at, CHANNELS:] = (tail * (1.0 / CUTOFF)).astype(kind)


LADDER = (1.0, 0.1353352832366127, 0.0024787521766663585, 6.14421235332821e-06)


def finish_kernel(count, *refs):
    keep_ref = refs[0]
    got_refs = refs[1 : 1 + count]
    direct_ref, w_env_ref, force_ref, grad_ref = refs[1 + count :]
    total = keep_ref[0]
    for got in got_refs:
        total = total + got[0].astype(F32)
    chan = total[:CHANNELS]
    high = chan.astype(BF16)
    low = (chan - high.astype(F32)).astype(BF16)
    both = jnp.concatenate([high, low], axis=0)
    w_env = w_env_ref[...]
    weights = jnp.concatenate([w_env, w_env], axis=1)
    part = lax.dot_general(both, weights, (((0,), (1,)), ((), ())), preferred_element_type=F32)
    grad_ref[0, 0, 0] = (direct_ref[...] + part).astype(BF16)
    force_ref[0, 0, 0] = -total[POS_ROW : POS_ROW + 3]


def shifted(value, axis, steps):
    count = lax.axis_size(axis)
    return lax.ppermute(value, axis, [(i, (i + steps) % count) for i in range(count)])


def gathered(value, axis):
    if lax.axis_size(axis) == 2:
        return [value, shifted(value, axis, 1)]
    return [value, shifted(value, axis, -1), shifted(value, axis, 1)]


def returned(parts, axis):
    if lax.axis_size(axis) == 2:
        return [shifted(parts[0], axis, 1)]
    return [shifted(parts[0], axis, 1), shifted(parts[1], axis, -1)]


VMEM = pl.BlockSpec(memory_space=pltpu.VMEM)
SMEM = pl.BlockSpec(memory_space=pltpu.SMEM)


def local(
    feats, positions, species, cell_counts, pair_list, w_env, radial, pair_scale, w_hidden,
    w_zero, w_one, w_out,
):
    sizes = [lax.axis_size(axis) for axis in ("gx", "gy", "gz")]
    nxu, nyu, nzu = [2 if size == 2 else 3 for size in sizes]
    cells = nxu * nyu * nzu
    msg = pl.pallas_call(
        pack_kernel,
        out_shape=jax.ShapeDtypeStruct((1, ROWS, SLOTS), BF16),
        in_specs=[SMEM, VMEM, VMEM, VMEM, VMEM],
        out_specs=VMEM,
        name="pack",
    )(cell_counts, feats, positions, species, w_env)
    block = jnp.concatenate(gathered(msg, "gy"), axis=0)
    block = jnp.concatenate(gathered(block, "gz"), axis=0)
    blocks = gathered(block, "gx")

    scale = jnp.pad(pair_scale, ((0, 2), (0, 2)))
    out_cells = nxu * nzu
    out_shape = [
        jax.ShapeDtypeStruct((1, 1, 1, SLOTS), F32),
        jax.ShapeDtypeStruct((SLOTS, D), F32),
        jax.ShapeDtypeStruct((out_cells, ROWS, SLOTS), F32),
    ] + [jax.ShapeDtypeStruct((out_cells, ROWS, SLOTS), BF16)] * (nyu - 1)
    scratch = [
        pltpu.SMEM((OFFSETS + 5,), jnp.int32),
        pltpu.VMEM((3, SLOTS, SLOTS), F32),
        pltpu.VMEM((cells + 1, SLOTS, SLOTS), F32),
        pltpu.VMEM((cells, 8, SLOTS), F32),
        pltpu.VMEM((cells, CHANNELS, SLOTS), BF16),
        pltpu.VMEM((PAIRS, QUAD, LANES), BF16),
        pltpu.VMEM((PAIRS, WIDE, LANES), BF16),
        pltpu.VMEM((PAIRS, SLOTS, LANES), F32),
        pltpu.VMEM((PAIRS, SLOTS, LANES), F32),
        pltpu.VMEM((PAIRS, SLOTS, LANES), F32),
        pltpu.VMEM((QUAD, WIDE), F32),
        pltpu.VMEM((QUAD, WIDE), F32),
        pltpu.VMEM((QUAD, WIDE), BF16),
        pltpu.VMEM((WIDE, QUAD), BF16),
        pltpu.VMEM((3, SLOTS, SLOTS), F32),
        pltpu.VMEM((cells, CHANNELS, SLOTS), F32),
        pltpu.VMEM((cells, 8, SLOTS), F32),
    ]
    results = pl.pallas_call(
        lambda *refs: main_kernel((nxu, nyu, nzu, sizes), *refs),
        out_shape=out_shape,
        in_specs=[SMEM] + [VMEM] * (nxu + 7),
        out_specs=[VMEM] * len(out_shape),
        scratch_shapes=scratch,
        name="pairs",
    )(
        pair_list, *blocks, feats, radial, scale, w_hidden, w_zero, w_one, w_out.reshape(1, D)
    )
    energy, direct, keep = results[:3]
    total = keep
    for got in returned(results[3:], "gy"):
        total = total + got.astype(F32)
    sends = [total[uz * nxu : (uz + 1) * nxu].astype(BF16) for uz in range(1, nzu)]
    total = total[:nxu]
    for got in returned(sends, "gz"):
        total = total + got.astype(F32)
    sends = [total[ux : ux + 1].astype(BF16) for ux in range(1, nxu)]
    keep = total[:1]
    arrived = returned(sends, "gx")
    forces, feat_grad = pl.pallas_call(
        lambda *refs: finish_kernel(len(arrived), *refs),
        out_shape=[
            jax.ShapeDtypeStruct((1, 1, 1, 3, SLOTS), F32),
            jax.ShapeDtypeStruct((1, 1, 1, SLOTS, D), BF16),
        ],
        in_specs=[VMEM] * (3 + len(arrived)),
        out_specs=[VMEM] * 2,
        name="finish",
    )(keep, *arrived, direct, w_env)
    return energy, forces, feat_grad


def solution(mesh):
    cell = P("gx", "gy", "gz")
    in_specs = (cell,) * 5 + (P(),) * 7
    return jax.shard_map(
        local, mesh=mesh, in_specs=in_specs, out_specs=(cell,) * 3, check_vma=False
    )
```

```python
import jax
import jax.numpy as jnp
from jax import lax
from jax.experimental import pallas as pl
from jax.experimental.pallas import tpu as pltpu
from jax.sharding import PartitionSpec as P

D = 256
CHANNELS = 64
NBASIS = 4
NSPEC = 6
SLOTS = 128
CUTOFF = 0.55
CENTRE = 0.5
ROWS = 80
POS_ROW = 64
CODE_ROW = 73
OFFSETS = 27
CHUNK = 16
CHUNKS = SLOTS // CHUNK
QUAD = NBASIS * SLOTS
WIDE = 4 * CHANNELS
LANES = 2 * SLOTS
PAIRS = (OFFSETS + 1) // 2
F32 = jnp.float32
BF16 = jnp.bfloat16


def dot_nn(a, b):
    return lax.dot_general(a, b, (((1,), (0,)), ((), ())), preferred_element_type=F32)


def dot_nt(a, b):
    return lax.dot_general(a, b, (((1,), (1,)), ((), ())), preferred_element_type=F32)


def split3(value):
    high = value.astype(BF16)
    rest = value - high.astype(F32)
    middle = rest.astype(BF16)
    low = (rest - middle.astype(F32)).astype(BF16)
    return high, middle, low


def pack_kernel(counts_ref, feats_ref, pos_ref, species_ref, w_env_ref, msg_ref):
    chans = dot_nt(w_env_ref[...], feats_ref[0, 0, 0])
    msg_ref[0, :CHANNELS] = chans.astype(BF16)
    pos = jnp.concatenate([pos_ref[0, 0, axis] for axis in range(3)], axis=0)
    slots = lax.broadcasted_iota(jnp.int32, (1, SLOTS), 1)
    counts = jnp.broadcast_to(counts_ref[0], (1, SLOTS))
    code = jnp.where(slots < counts, species_ref[0, 0].astype(F32), -1.0)
    high = pos.astype(BF16).astype(F32)
    middle = (pos - high).astype(BF16).astype(F32)
    low = pos - high - middle
    tail = jnp.concatenate([high, middle, low, code, jnp.zeros((6, SLOTS), F32)], axis=0)
    msg_ref[0, CHANNELS:] = tail.astype(BF16)


def unique_of(offset, count):
    if offset == 0 or count == 2:
        return abs(offset)
    return 1 if offset > 0 else 2


def main_kernel(shape, *refs):
    nxu, nyu, nzu, sizes = shape
    cells = nxu * nyu * nzu
    refs = list(refs)
    list_ref = refs.pop(0)
    msg_refs = [refs.pop(0) for _ in range(nxu)]
    (feats_ref, radial_ref, scale_ref, w_hidden_ref, w_zero_ref, w_one_ref, w_out_ref) = refs[:7]
    refs = refs[7:]
    energy_ref, direct_ref = refs[:2]
    out_refs = refs[2 : 2 + nyu]
    (
        cell_of, slot_of, shift_of, xi, weight, xj, chan, tiles, rmat, s_all, r_all, wb_all,
        acc, pbuf, grad, gradt, fi, cg, pg,
    ) = refs[2 + nyu :]

    live = jnp.int32(0)
    for tile in range(OFFSETS):
        offset = (tile // 9 - 1, tile // 3 % 3 - 1, tile % 3 - 1)
        ux, uy, uz = [unique_of(o, size) for o, size in zip(offset, sizes)]
        cell = (ux * nzu + uz) * nyu + uy
        cell_of[live] = jnp.int32(cell)
        slot_of[live] = jnp.int32(cell)
        for axis in range(3):
            shift_of[axis, live] = jnp.float32(offset[axis] / CUTOFF)
        live = live + list_ref[0, 0, 0, tile]
    cell_of[live] = jnp.int32(0)
    slot_of[live] = jnp.int32(cells)
    for axis in range(3):
        shift_of[axis, live] = jnp.float32(0.0)
    trips = (live + 1) // 2

    code_rows = []
    for cell in range(cells):
        msg = msg_refs[cell // (nyu * nzu)]
        at = cell % (nyu * nzu)
        tail = msg[at, CHANNELS:].astype(F32)
        place = tail[0:3] + tail[3:6] + tail[6:9]
        xj[cell, 0:3] = (place - CENTRE) * (1.0 / CUTOFF)
        code_rows.append(tail[9:10])
        chan[cell] = msg[at, :CHANNELS]
        cg[cell] = jnp.zeros((CHANNELS, SLOTS), F32)
        pg[cell] = jnp.zeros((8, SLOTS), F32)
    for axis in range(3):
        row = jnp.broadcast_to(xj[0, axis : axis + 1], (SLOTS, SLOTS))
        xi[axis] = row.T
    code_i = jnp.broadcast_to(code_rows[0], (SLOTS, SLOTS)).T
    lane = lax.broadcasted_iota(jnp.int32, (SLOTS, SLOTS), 1)
    sub = lax.broadcasted_iota(jnp.int32, (SLOTS, SLOTS), 0)
    onehot = jnp.where((code_i == (lane % 8).astype(F32)) & (lane < 24), 1.0, 0.0)
    onehot = onehot.astype(BF16)
    scale = jnp.concatenate([scale_ref[...], jnp.zeros((8 - NSPEC, NSPEC), F32)], axis=0)
    coef = []
    for cell in range(cells):
        total = jnp.zeros((8, SLOTS), F32)
        for kind in range(NSPEC):
            column = jnp.broadcast_to(scale[:, kind : kind + 1], (8, SLOTS))
            total = total + jnp.where(code_rows[cell] == float(kind), column, 0.0)
        high = total.astype(BF16).astype(F32)
        middle = (total - high).astype(BF16).astype(F32)
        low = total - high - middle
        coef.append(
            jnp.concatenate([high, middle, low, jnp.zeros((104, SLOTS), F32)], axis=0).astype(BF16)
        )
    for cell in range(0, cells, 2):
        strength = dot_nn(onehot, jnp.concatenate(coef[cell : cell + 2], axis=1))
        first = strength[:, :SLOTS]
        weight[cell] = jnp.where(lane == sub, 0.0, first) if cell == 0 else first
        if cell + 1 < cells:
            weight[cell + 1] = strength[:, SLOTS:]
    weight[cells] = jnp.zeros((SLOTS, SLOTS), F32)
    acc[...] = jnp.zeros_like(acc)
    fi[...] = jnp.zeros_like(fi)

    def rows_of(pair):
        first, second = 2 * pair, 2 * pair + 1
        cell_a, cell_b = cell_of[first], cell_of[second]
        rows = [
            jnp.concatenate(
                [
                    xj[cell_a, axis : axis + 1] + shift_of[axis, first],
                    xj[cell_b, axis : axis + 1] + shift_of[axis, second],
                ],
                axis=1,
            )
            for axis in range(3)
        ]
        return cell_a, cell_b, slot_of[first], slot_of[second], rows

    def relative(rows, block):
        out = []
        for axis in range(3):
            own = xi[axis, block * CHUNK : (block + 1) * CHUNK]
            out.append(rows[axis] - jnp.concatenate([own, own], axis=1))
        return out

    def forward(pair, carry):
        cell_a, cell_b, weight_a, weight_b, rows = rows_of(pair)
        values = jnp.concatenate([chan[cell_a], chan[cell_b]], axis=1)
        rmat[pair, :CHANNELS] = values
        wide = values.astype(F32)
        for axis in range(3):
            base = (axis + 1) * CHANNELS
            rmat[pair, base : base + CHANNELS] = (wide * rows[axis]).astype(BF16)
        for block in range(CHUNKS):
            at = slice(block * CHUNK, (block + 1) * CHUNK)
            dx, dy, dz = relative(rows, block)
            s = jnp.minimum(dx * dx + dy * dy + dz * dz, 1.0)
            inside = 1.0 - s
            spread = 4.0 * s - 0.5
            ratio = jnp.exp(8.0 * s)
            strength = jnp.concatenate([weight[weight_a, at], weight[weight_b, at]], axis=1)
            wb = strength * jnp.exp(-(spread * spread))
            s_all[pair, at] = s
            r_all[pair, at] = ratio
            wb_all[pair, at] = wb
            tile = wb * (inside * inside)
            for k in range(NBASIS):
                base = block * 4 * CHUNK + k * CHUNK
                tiles[pair, base : base + CHUNK] = tile.astype(BF16)
                if k + 1 < NBASIS:
                    tile = tile * ratio
        acc[...] += dot_nt(tiles[pair], rmat[pair])
        return carry

    lax.fori_loop(0, trips, forward, 0)

    radial = radial_ref[...]
    weights_k = []
    for k in range(NBASIS):
        row = radial[k : k + 1] * LADDER[k]
        weights_k.append(jnp.concatenate([row] * 4, axis=1))
    mixed = []
    for block in range(CHUNKS):
        base = block * 4 * CHUNK
        total = weights_k[0] * acc[base : base + CHUNK]
        for k in range(1, NBASIS):
            total = total + weights_k[k] * acc[base + k * CHUNK : base + (k + 1) * CHUNK]
        mixed.append(total)
    mixed = jnp.concatenate(mixed, axis=0)
    scalar = mixed[:, :CHANNELS]
    vectors = [
        mixed[:, (axis + 1) * CHANNELS : (axis + 2) * CHANNELS] - xi[axis][:, :CHANNELS] * scalar
        for axis in range(3)
    ]
    norms = vectors[0] * vectors[0] + vectors[1] * vectors[1] + vectors[2] * vectors[2]
    pre = dot_nn(feats_ref[0, 0, 0], w_hidden_ref[...])
    pre = pre + dot_nn(scalar.astype(BF16), w_zero_ref[...])
    pre = pre + dot_nn(norms.astype(BF16), w_one_ref[...])
    gate = jax.nn.sigmoid(pre)
    w_out = w_out_ref[...]
    occupied = code_i >= 0.0
    energy = jnp.sum(pre * gate * w_out, axis=1, keepdims=True)
    energy = jnp.where(occupied, jnp.broadcast_to(energy, (SLOTS, SLOTS)), 0.0).T
    energy_ref[0, 0] = energy[0:1]
    occupied_wide = jnp.concatenate([occupied, occupied], axis=1)
    pre_grad = jnp.where(occupied_wide, w_out * gate * (1.0 + pre * (1.0 - gate)), 0.0)
    pre_grad = pre_grad.astype(BF16)
    direct_ref[...] = dot_nt(pre_grad, w_hidden_ref[...])
    zero_grad = dot_nt(pre_grad, w_zero_ref[...])
    one_grad = 2.0 * dot_nt(pre_grad, w_one_ref[...])
    parts = [vector * one_grad for vector in vectors]
    own_force = [jnp.sum(part * scalar, axis=1, keepdims=True) for part in parts]
    head = zero_grad
    for axis in range(3):
        head = head - xi[axis][:, :CHANNELS] * parts[axis]
    full = jnp.concatenate([head] + parts, axis=1)
    for block in range(CHUNKS):
        piece = full[block * CHUNK : (block + 1) * CHUNK]
        for k in range(NBASIS):
            base = block * 4 * CHUNK + k * CHUNK
            scaled = weights_k[k] * piece
            grad[base : base + CHUNK] = scaled.astype(BF16)
    place = lax.broadcasted_iota(jnp.int32, (WIDE, WIDE), 0)
    held = place % CHUNK + place // (4 * CHUNK) * CHUNK + place // CHUNK % 4 * CHANNELS
    picked = lax.broadcasted_iota(jnp.int32, (WIDE, WIDE), 1) == held
    gradt[...] = dot_nt(jnp.where(picked, 1.0, 0.0).astype(BF16), grad[...]).astype(BF16)

    def backward(pair, carry):
        cell_a, cell_b, weight_a, weight_b, rows = rows_of(pair)
        pbuf[...] = dot_nn(grad[...], rmat[pair])
        back = dot_nn(gradt[...], tiles[pair])
        along = [jnp.zeros((CHUNK, LANES), F32) for _ in range(3)]
        for part in range(CHANNELS // CHUNK):
            at = slice(part * CHUNK, (part + 1) * CHUNK)
            values = rmat[pair, at].astype(F32)
            sums = back[part * 4 * CHUNK : part * 4 * CHUNK + CHUNK]
            for axis in range(3):
                base = part * 4 * CHUNK + (axis + 1) * CHUNK
                piece = back[base : base + CHUNK]
                sums = sums + rows[axis] * piece
                along[axis] = along[axis] + values * piece
            cg[cell_a, at] += sums[:, :SLOTS]
            cg[cell_b, at] += sums[:, SLOTS:]
        totals = [jnp.zeros((CHUNK, LANES), F32) for _ in range(3)]
        for block in range(CHUNKS):
            at = slice(block * CHUNK, (block + 1) * CHUNK)
            s = s_all[pair, at]
            ratio = r_all[pair, at]
            inside = 1.0 - s
            step = 8.0 * inside
            level = -2.0 - step * (4.0 * s - 0.5)
            levels = [level]
            for k in range(1, NBASIS):
                levels.append(levels[-1] + step)
            base = block * 4 * CHUNK
            slope = levels[3] * pbuf[base + 3 * CHUNK : base + 4 * CHUNK]
            for k in (2, 1, 0):
                slope = slope * ratio + levels[k] * pbuf[base + k * CHUNK : base + (k + 1) * CHUNK]
            slope = slope * (wb_all[pair, at] * inside)
            for axis, delta in enumerate(relative(rows, block)):
                push = slope * delta
                totals[axis] = totals[axis] + push
                fi[axis, at] += push[:, :SLOTS] + push[:, SLOTS:]
        for axis in range(3):
            total = jnp.sum(totals[axis] * 2.0 + along[axis], axis=0, keepdims=True)
            pg[cell_a, axis : axis + 1] += total[:, :SLOTS]
            pg[cell_b, axis : axis + 1] += total[:, SLOTS:]
        return carry

    lax.fori_loop(0, trips, backward, 0)

    for axis in range(3):
        column = jnp.sum(fi[axis], axis=1, keepdims=True) * 2.0 + own_force[axis]
        row = jnp.broadcast_to(column, (SLOTS, SLOTS)).T
        pg[0, axis : axis + 1] -= row[0:1]
    for uy in range(nyu):
        for uz in range(nzu):
            for ux in range(nxu):
                cell = (ux * nzu + uz) * nyu + uy
                kind = out_refs[uy].dtype
                at = uz * nxu + ux
                out_refs[uy][at, :CHANNELS] = cg[cell].astype(kind)
                tail = jnp.concatenate([pg[cell], jnp.zeros((8, SLOTS), F32)], axis=0)
                out_refs[uy][at, CHANNELS:] = (tail * (1.0 / CUTOFF)).astype(kind)


LADDER = (1.0, 0.1353352832366127, 0.0024787521766663585, 6.14421235332821e-06)


def finish_kernel(count, *refs):
    keep_ref = refs[0]
    got_refs = refs[1 : 1 + count]
    direct_ref, w_env_ref, force_ref, grad_ref = refs[1 + count :]
    total = keep_ref[0]
    for got in got_refs:
        total = total + got[0].astype(F32)
    chan = total[:CHANNELS]
    high = chan.astype(BF16)
    low = (chan - high.astype(F32)).astype(BF16)
    both = jnp.concatenate([high, low], axis=0)
    w_env = w_env_ref[...]
    weights = jnp.concatenate([w_env, w_env], axis=0)
    part = lax.dot_general(both, weights, (((0,), (0,)), ((), ())), preferred_element_type=F32)
    grad_ref[0, 0, 0] = (direct_ref[...] + part).astype(BF16)
    for axis in range(3):
        force_ref[0, 0, axis] = -total[POS_ROW + axis : POS_ROW + axis + 1]


def shifted(value, axis, steps):
    count = lax.axis_size(axis)
    return lax.ppermute(value, axis, [(i, (i + steps) % count) for i in range(count)])


def gathered(value, axis):
    if lax.axis_size(axis) == 2:
        return [value, shifted(value, axis, 1)]
    return [value, shifted(value, axis, -1), shifted(value, axis, 1)]


def returned(parts, axis):
    if lax.axis_size(axis) == 2:
        return [shifted(parts[0], axis, 1)]
    return [shifted(parts[0], axis, 1), shifted(parts[1], axis, -1)]


VMEM = pl.BlockSpec(memory_space=pltpu.VMEM)
SMEM = pl.BlockSpec(memory_space=pltpu.SMEM)
SMALL = pltpu.CompilerParams(vmem_limit_bytes=4 << 20)


def local(
    feats, positions, species, cell_counts, pair_list, w_env, radial, pair_scale, w_hidden,
    w_zero, w_one, w_out,
):
    sizes = [lax.axis_size(axis) for axis in ("gx", "gy", "gz")]
    nxu, nyu, nzu = [2 if size == 2 else 3 for size in sizes]
    cells = nxu * nyu * nzu
    msg = pl.pallas_call(
        pack_kernel,
        out_shape=jax.ShapeDtypeStruct((1, ROWS, SLOTS), BF16),
        in_specs=[VMEM] * 5,
        out_specs=VMEM,
        name="pack",
    )(cell_counts, feats, positions.transpose(0, 1, 3, 2, 4), species, w_env.T)
    block = jnp.concatenate(gathered(msg, "gy"), axis=0)
    block = jnp.concatenate(gathered(block, "gz"), axis=0)
    blocks = gathered(block, "gx")

    out_cells = nxu * nzu
    out_shape = [
        jax.ShapeDtypeStruct((1, 1, 1, SLOTS), F32),
        jax.ShapeDtypeStruct((SLOTS, D), F32),
        jax.ShapeDtypeStruct((out_cells, ROWS, SLOTS), F32),
    ] + [jax.ShapeDtypeStruct((out_cells, ROWS, SLOTS), BF16)] * (nyu - 1)
    scratch = [
        pltpu.SMEM((OFFSETS + 5,), jnp.int32),
        pltpu.SMEM((OFFSETS + 5,), jnp.int32),
        pltpu.SMEM((3, OFFSETS + 5), F32),
        pltpu.VMEM((3, SLOTS, SLOTS), F32),
        pltpu.VMEM((cells + 1, SLOTS, SLOTS), F32),
        pltpu.VMEM((cells, 8, SLOTS), F32),
        pltpu.VMEM((cells, CHANNELS, SLOTS), BF16),
        pltpu.VMEM((PAIRS, QUAD, LANES), BF16),
        pltpu.VMEM((PAIRS, WIDE, LANES), BF16),
        pltpu.VMEM((PAIRS, SLOTS, LANES), F32),
        pltpu.VMEM((PAIRS, SLOTS, LANES), F32),
        pltpu.VMEM((PAIRS, SLOTS, LANES), F32),
        pltpu.VMEM((QUAD, WIDE), F32),
        pltpu.VMEM((QUAD, WIDE), F32),
        pltpu.VMEM((QUAD, WIDE), BF16),
        pltpu.VMEM((WIDE, QUAD), BF16),
        pltpu.VMEM((3, SLOTS, SLOTS), F32),
        pltpu.VMEM((cells, CHANNELS, SLOTS), F32),
        pltpu.VMEM((cells, 8, SLOTS), F32),
    ]
    results = pl.pallas_call(
        lambda *refs: main_kernel((nxu, nyu, nzu, sizes), *refs),
        out_shape=out_shape,
        in_specs=[SMEM] + [VMEM] * (nxu + 7),
        out_specs=[VMEM] * len(out_shape),
        scratch_shapes=scratch,
        compiler_params=pltpu.CompilerParams(vmem_limit_bytes=24 << 20),
        name="pairs",
    )(
        pair_list, *blocks, feats, radial, pair_scale, w_hidden, w_zero, w_one, w_out.reshape(1, D)
    )
    energy, direct, keep = results[:3]
    total = keep
    for got in returned(results[3:], "gy"):
        total = total + got.astype(F32)
    sends = [total[uz * nxu : (uz + 1) * nxu].astype(BF16) for uz in range(1, nzu)]
    total = total[:nxu]
    for got in returned(sends, "gz"):
        total = total + got.astype(F32)
    sends = [total[ux : ux + 1].astype(BF16) for ux in range(1, nxu)]
    keep = total[:1]
    arrived = returned(sends, "gx")
    forces, feat_grad = pl.pallas_call(
        lambda *refs: finish_kernel(len(arrived), *refs),
        out_shape=[
            jax.ShapeDtypeStruct((1, 1, 3, 1, SLOTS), F32),
            jax.ShapeDtypeStruct((1, 1, 1, SLOTS, D), BF16),
        ],
        in_specs=[VMEM] * (3 + len(arrived)),
        out_specs=[VMEM] * 2,
        compiler_params=SMALL,
        name="finish",
    )(keep, *arrived, direct, w_env.T)
    return energy, forces.transpose(0, 1, 3, 2, 4), feat_grad


def solution(mesh):
    cell = P("gx", "gy", "gz")
    in_specs = (cell,) * 5 + (P(),) * 7
    return jax.shard_map(
        local, mesh=mesh, in_specs=in_specs, out_specs=(cell,) * 3, check_vma=False
    )
```

```python
import jax
import jax.numpy as jnp
from jax import lax
from jax.experimental import pallas as pl
from jax.experimental.pallas import tpu as pltpu
from jax.sharding import PartitionSpec as P


D = 256
CHANNELS = 64
NBASIS = 4
NSPEC = 6
SLOTS = 128
CUTOFF = 0.55
CENTRE = 0.5
ROWS = 80
POS_ROW = 64
OFFSETS = 27
CHUNK = 16
CHUNKS = SLOTS // CHUNK
QUAD = NBASIS * SLOTS
WIDE = 4 * CHANNELS
LANES = 2 * SLOTS
PAIRS = (OFFSETS + 1) // 2
F32 = jnp.float32
BF16 = jnp.bfloat16


def dot_nn(a, b):
    return lax.dot_general(a, b, (((1,), (0,)), ((), ())), preferred_element_type=F32)


def dot_nt(a, b):
    return lax.dot_general(a, b, (((1,), (1,)), ((), ())), preferred_element_type=F32)


def split3(value):
    high = value.astype(BF16)
    rest = value - high.astype(F32)
    middle = rest.astype(BF16)
    low = (rest - middle.astype(F32)).astype(BF16)
    return high, middle, low


def pack_kernel(counts_ref, feats_ref, pos_ref, species_ref, w_env_ref, msg_ref):
    chans = dot_nt(w_env_ref[...], feats_ref[0, 0, 0])
    msg_ref[0, :CHANNELS] = chans.astype(BF16)
    pos = jnp.concatenate([pos_ref[0, 0, axis] for axis in range(3)], axis=0)
    slots = lax.broadcasted_iota(jnp.int32, (1, SLOTS), 1)
    counts = jnp.broadcast_to(counts_ref[0], (1, SLOTS))
    code = jnp.where(slots < counts, species_ref[0, 0].astype(F32), -1.0)
    high = pos.astype(BF16).astype(F32)
    middle = (pos - high).astype(BF16).astype(F32)
    low = pos - high - middle
    tail = jnp.concatenate([high, middle, low, code, jnp.zeros((6, SLOTS), F32)], axis=0)
    msg_ref[0, CHANNELS:] = tail.astype(BF16)


def row_sums(value):
    ones = jnp.ones((8, value.shape[1]), BF16)
    high, middle, low = split3(value)
    total = dot_nt(ones, high) + dot_nt(ones, middle) + dot_nt(ones, low)
    return total[0:1]


def unique_of(offset, count):
    if offset == 0 or count == 2:
        return abs(offset)
    return 1 if offset > 0 else 2


def main_kernel(shape, *refs):
    nxu, nyu, nzu, sizes = shape
    cells = nxu * nyu * nzu
    refs = list(refs)
    list_ref = refs.pop(0)
    msg_refs = [refs.pop(0) for _ in range(nxu)]
    (
        feats_ref, radial_ref, scale_ref, w_hidden_ref, w_zero_ref, w_one_ref, w_out_ref, swap_ref,
    ) = refs[:8]
    refs = refs[8:]
    energy_ref, direct_ref = refs[:2]
    out_refs = refs[2 : 2 + nyu]
    (
        cell_of, slot_of, shift_of, xi, weight, xj, chan, tiles, rmat, s_all, r_all, wb_all,
        acc, pbuf, bbuf, hbuf, tile_now, rmat_now, grad, gradt, fi, cg, pg,
    ) = refs[2 + nyu :]

    live = jnp.int32(0)
    for tile in range(OFFSETS):
        offset = (tile // 9 - 1, tile // 3 % 3 - 1, tile % 3 - 1)
        ux, uy, uz = [unique_of(o, size) for o, size in zip(offset, sizes)]
        cell = (ux * nzu + uz) * nyu + uy
        cell_of[live] = jnp.int32(cell)
        slot_of[live] = jnp.int32(cell)
        for axis in range(3):
            shift_of[axis, live] = jnp.float32(offset[axis] / CUTOFF)
        live = live + list_ref[0, 0, 0, tile]
    cell_of[live] = jnp.int32(0)
    slot_of[live] = jnp.int32(cells)
    for axis in range(3):
        shift_of[axis, live] = jnp.float32(0.0)
    trips = (live + 1) // 2
    hbuf[...] = dot_nn(feats_ref[0, 0, 0], w_hidden_ref[...])

    code_rows = []
    for cell in range(cells):
        msg = msg_refs[cell // (nyu * nzu)]
        at = cell % (nyu * nzu)
        tail = msg[at, CHANNELS:].astype(F32)
        place = tail[0:3] + tail[3:6] + tail[6:9]
        xj[cell, 0:3] = (place - CENTRE) * (1.0 / CUTOFF)
        code_rows.append(tail[9:10])
        chan[cell] = msg[at, :CHANNELS]
        cg[cell] = jnp.zeros((CHANNELS, SLOTS), F32)
        pg[cell] = jnp.zeros((8, SLOTS), F32)
    for axis in range(3):
        row = jnp.broadcast_to(xj[0, axis : axis + 1], (SLOTS, SLOTS))
        xi[axis] = row.T
    code_i = jnp.broadcast_to(code_rows[0], (SLOTS, SLOTS)).T
    lane = lax.broadcasted_iota(jnp.int32, (SLOTS, SLOTS), 1)
    sub = lax.broadcasted_iota(jnp.int32, (SLOTS, SLOTS), 0)
    onehot = jnp.where((code_i == (lane % 8).astype(F32)) & (lane < 24), 1.0, 0.0)
    onehot = onehot.astype(BF16)
    scale = jnp.concatenate([scale_ref[...], jnp.zeros((8 - NSPEC, NSPEC), F32)], axis=0)
    coef = []
    for cell in range(cells):
        total = jnp.zeros((8, SLOTS), F32)
        for kind in range(NSPEC):
            column = jnp.broadcast_to(scale[:, kind : kind + 1], (8, SLOTS))
            total = total + jnp.where(code_rows[cell] == float(kind), column, 0.0)
        high = total.astype(BF16).astype(F32)
        middle = (total - high).astype(BF16).astype(F32)
        low = total - high - middle
        coef.append(
            jnp.concatenate([high, middle, low, jnp.zeros((104, SLOTS), F32)], axis=0).astype(BF16)
        )
    for cell in range(0, cells, 2):
        strength = dot_nn(onehot, jnp.concatenate(coef[cell : cell + 2], axis=1))
        first = strength[:, :SLOTS]
        weight[cell] = jnp.where(lane == sub, 0.0, first) if cell == 0 else first
        if cell + 1 < cells:
            weight[cell + 1] = strength[:, SLOTS:]
    weight[cells] = jnp.zeros((SLOTS, SLOTS), F32)
    acc[...] = jnp.zeros_like(acc)
    tile_now[...] = jnp.zeros_like(tile_now)
    rmat_now[...] = jnp.zeros_like(rmat_now)

    def rows_of(pair):
        first, second = 2 * pair, 2 * pair + 1
        cell_a, cell_b = cell_of[first], cell_of[second]
        rows = [
            jnp.concatenate(
                [
                    xj[cell_a, axis : axis + 1] + shift_of[axis, first],
                    xj[cell_b, axis : axis + 1] + shift_of[axis, second],
                ],
                axis=1,
            )
            for axis in range(3)
        ]
        return cell_a, cell_b, slot_of[first], slot_of[second], rows

    def relative(rows, block):
        out = []
        for axis in range(3):
            own = xi[axis, block * CHUNK : (block + 1) * CHUNK]
            out.append(rows[axis] - jnp.concatenate([own, own], axis=1))
        return out

    def forward(pair, carry):
        acc[...] += dot_nt(tile_now[...], rmat_now[...])
        cell_a, cell_b, weight_a, weight_b, rows = rows_of(pair)
        for block in range(CHUNKS):
            at = slice(block * CHUNK, (block + 1) * CHUNK)
            dx, dy, dz = relative(rows, block)
            s = jnp.minimum(dx * dx + dy * dy + dz * dz, 1.0)
            inside = 1.0 - s
            spread = 4.0 * s - 0.5
            ratio = jnp.exp(8.0 * s)
            strength = jnp.concatenate([weight[weight_a, at], weight[weight_b, at]], axis=1)
            wb = strength * jnp.exp(-(spread * spread))
            s_all[pair, at] = s
            r_all[pair, at] = ratio
            wb_all[pair, at] = wb
            tile = wb * (inside * inside)
            for k in range(NBASIS):
                base = block * 4 * CHUNK + k * CHUNK
                rounded = tile.astype(BF16)
                tiles[pair, base : base + CHUNK] = rounded
                tile_now[base : base + CHUNK] = rounded
                if k + 1 < NBASIS:
                    tile = tile * ratio
        values = jnp.concatenate([chan[cell_a], chan[cell_b]], axis=1)
        rmat[pair, :CHANNELS] = values
        rmat_now[:CHANNELS] = values
        wide = values.astype(F32)
        for axis in range(3):
            base = (axis + 1) * CHANNELS
            scaled = (wide * rows[axis]).astype(BF16)
            rmat[pair, base : base + CHANNELS] = scaled
            rmat_now[base : base + CHANNELS] = scaled
        return carry

    lax.fori_loop(0, trips, forward, 0)
    acc[...] += dot_nt(tile_now[...], rmat_now[...])

    radial = radial_ref[...]
    weights_k = []
    for k in range(NBASIS):
        row = radial[k : k + 1] * LADDER[k]
        weights_k.append(jnp.concatenate([row] * 4, axis=1))
    mixed = []
    for block in range(CHUNKS):
        base = block * 4 * CHUNK
        total = weights_k[0] * acc[base : base + CHUNK]
        for k in range(1, NBASIS):
            total = total + weights_k[k] * acc[base + k * CHUNK : base + (k + 1) * CHUNK]
        mixed.append(total)
    mixed = jnp.concatenate(mixed, axis=0)
    low = lane < CHANNELS
    left, right = mixed[:, :SLOTS], mixed[:, SLOTS:]
    scalar = jnp.where(low, left, pltpu.roll(left, CHANNELS, 1))
    own_left = jnp.where(low, 0.0, xi[0])
    own_right = jnp.where(low, xi[1], xi[2])
    left = left - own_left * scalar
    right = right - own_right * scalar
    features = [jnp.where(low, left, left * left), right * right]
    features = jnp.concatenate(features, axis=1).astype(BF16)
    w_one = w_one_ref[...]
    w_all = jnp.concatenate([w_zero_ref[...], w_one, w_one, w_one], axis=0)
    pre = hbuf[...] + dot_nn(features, w_all)
    gate = jax.nn.sigmoid(pre)
    occupied = jnp.concatenate([code_i, code_i], axis=1) >= 0.0
    w_out = jnp.where(occupied, w_out_ref[...], 0.0)
    pre_grad = (w_out * gate * (1.0 + pre * (1.0 - gate))).astype(BF16)
    back_all = dot_nt(pre_grad, w_all)
    back_left, back_right = back_all[:, :SLOTS], back_all[:, SLOTS:]
    part_left = jnp.where(low, back_left, 2.0 * left * back_left)
    part_right = 2.0 * right * back_right
    fold = own_left * part_left + own_right * part_right
    fold = fold + pltpu.roll(fold, CHANNELS, 1)
    full = jnp.concatenate([part_left - jnp.where(low, fold, 0.0), part_right], axis=1)
    half = 0.5 * scalar
    fi[0] = jnp.where(low, 0.0, half * part_left)
    fi[1] = jnp.where(low, half * part_right, 0.0)
    fi[2] = jnp.where(low, 0.0, half * part_right)
    for block in range(CHUNKS):
        piece = full[block * CHUNK : (block + 1) * CHUNK]
        for k in range(NBASIS):
            base = block * 4 * CHUNK + k * CHUNK
            scaled = weights_k[k] * piece
            grad[base : base + CHUNK] = scaled.astype(BF16)
    pbuf[...] = dot_nn(grad[...], rmat[0])
    gradt[...] = dot_nt(swap_ref[...], grad[...]).astype(BF16)
    energy_ref[0, 0] = row_sums(pre * gate * w_out)
    direct_ref[...] = dot_nt(pre_grad, w_hidden_ref[...])

    def backward(pair, carry):
        cell_a, cell_b, _, _, rows = rows_of(pair)
        bbuf[...] = dot_nn(gradt[...], tiles[pair])
        totals = [jnp.zeros((CHUNK, LANES), F32) for _ in range(3)]
        for block in range(CHUNKS):
            at = slice(block * CHUNK, (block + 1) * CHUNK)
            s = s_all[pair, at]
            ratio = r_all[pair, at]
            inside = 1.0 - s
            step = 8.0 * inside
            level = -2.0 - step * (4.0 * s - 0.5)
            levels = [level]
            for _ in range(1, NBASIS):
                levels.append(levels[-1] + step)
            base = block * 4 * CHUNK
            slope = levels[3] * pbuf[base + 3 * CHUNK : base + 4 * CHUNK]
            for k in (2, 1, 0):
                slope = slope * ratio + levels[k] * pbuf[base + k * CHUNK : base + (k + 1) * CHUNK]
            slope = slope * (wb_all[pair, at] * inside)
            for axis, delta in enumerate(relative(rows, block)):
                push = slope * delta
                totals[axis] = totals[axis] + push
                fi[axis, at] += push[:, :SLOTS] + push[:, SLOTS:]
        pbuf[...] = dot_nn(grad[...], rmat[pair + 1])
        totals = [2.0 * total for total in totals]
        for part in range(CHANNELS // CHUNK):
            at = slice(part * CHUNK, (part + 1) * CHUNK)
            values = rmat[pair, at].astype(F32)
            sums = bbuf[part * 4 * CHUNK : part * 4 * CHUNK + CHUNK]
            for axis in range(3):
                base = part * 4 * CHUNK + (axis + 1) * CHUNK
                piece = bbuf[base : base + CHUNK]
                sums = sums + rows[axis] * piece
                totals[axis] = totals[axis] + values * piece
            cg[cell_a, at] += sums[:, :SLOTS]
            cg[cell_b, at] += sums[:, SLOTS:]
        for axis in range(3):
            total = jnp.sum(totals[axis], axis=0, keepdims=True)
            pg[cell_a, axis : axis + 1] += total[:, :SLOTS]
            pg[cell_b, axis : axis + 1] += total[:, SLOTS:]
        return carry

    lax.fori_loop(0, trips, backward, 0)

    for axis in range(3):
        pg[0, axis : axis + 1] -= 2.0 * row_sums(fi[axis])
    for uy in range(nyu):
        for uz in range(nzu):
            for ux in range(nxu):
                cell = (ux * nzu + uz) * nyu + uy
                kind = out_refs[uy].dtype
                at = uz * nxu + ux
                out_refs[uy][at, :CHANNELS] = cg[cell].astype(kind)
                tail = jnp.concatenate([pg[cell], jnp.zeros((8, SLOTS), F32)], axis=0)
                out_refs[uy][at, CHANNELS:] = (tail * (1.0 / CUTOFF)).astype(kind)


LADDER = (1.0, 0.1353352832366127, 0.0024787521766663585, 6.14421235332821e-06)


def finish_kernel(count, *refs):
    keep_ref = refs[0]
    got_refs = refs[1 : 1 + count]
    direct_ref, w_env_ref, force_ref, grad_ref = refs[1 + count :]
    total = keep_ref[0]
    for got in got_refs:
        total = total + got[0].astype(F32)
    chan = total[:CHANNELS]
    high = chan.astype(BF16)
    low = (chan - high.astype(F32)).astype(BF16)
    both = jnp.concatenate([high, low], axis=0)
    w_env = w_env_ref[...]
    weights = jnp.concatenate([w_env, w_env], axis=0)
    part = lax.dot_general(both, weights, (((0,), (0,)), ((), ())), preferred_element_type=F32)
    grad_ref[0, 0, 0] = (direct_ref[...] + part).astype(BF16)
    for axis in range(3):
        force_ref[0, 0, axis] = -total[POS_ROW + axis : POS_ROW + axis + 1]


def shifted(value, axis, steps):
    count = lax.axis_size(axis)
    return lax.ppermute(value, axis, [(i, (i + steps) % count) for i in range(count)])


def gathered(value, axis):
    if lax.axis_size(axis) == 2:
        return [value, shifted(value, axis, 1)]
    up = shifted(value, axis, -1)
    down = shifted(value, axis, 1)
    return [value, up, down]


def returned(parts, axis):
    count = lax.axis_size(axis)
    if count == 2:
        return [shifted(parts[0], axis, 1)]
    if count % 2:
        return [shifted(parts[1], axis, -1), shifted(parts[0], axis, 1)]
    even = lax.axis_index(axis) % 2 == 0
    near = jnp.where(even, parts[0], parts[1])
    far = jnp.where(even, parts[1], parts[0])
    ring = [(i, (((i + 1) % count) ^ 1) - 1) for i in range(count)]
    ring = [(source, target % count) for source, target in ring]
    far = lax.ppermute(far, axis, ring)
    near = lax.ppermute(near, axis, [(i, i ^ 1) for i in range(count)])
    return [far, near]


VMEM = pl.BlockSpec(memory_space=pltpu.VMEM)
SMEM = pl.BlockSpec(memory_space=pltpu.SMEM)
SMALL = pltpu.CompilerParams(vmem_limit_bytes=4 << 20)


def layer(
    feats, positions, species, cell_counts, pair_list, w_env, radial, pair_scale, w_hidden,
    w_zero, w_one, w_out,
):
    sizes = [lax.axis_size(axis) for axis in ("gx", "gy", "gz")]
    nxu, nyu, nzu = [2 if size == 2 else 3 for size in sizes]
    cells = nxu * nyu * nzu
    msg = pl.pallas_call(
        pack_kernel,
        out_shape=jax.ShapeDtypeStruct((1, ROWS, SLOTS), BF16),
        in_specs=[VMEM] * 5,
        out_specs=VMEM,
        name="pack",
    )(cell_counts, feats, positions.transpose(0, 1, 3, 2, 4), species, w_env.T)
    block = jnp.concatenate(gathered(msg, "gy"), axis=0)
    block = jnp.concatenate(gathered(block, "gz"), axis=0)
    blocks = gathered(block, "gx")

    place = jnp.arange(WIDE)
    held = place % CHUNK + place // (4 * CHUNK) * CHUNK + place // CHUNK % 4 * CHANNELS
    swap = (held[:, None] == place[None, :]).astype(BF16)
    out_cells = nxu * nzu
    out_shape = [
        jax.ShapeDtypeStruct((1, 1, 1, SLOTS), F32),
        jax.ShapeDtypeStruct((SLOTS, D), F32),
        jax.ShapeDtypeStruct((out_cells, ROWS, SLOTS), F32),
    ] + [jax.ShapeDtypeStruct((out_cells, ROWS, SLOTS), BF16)] * (nyu - 1)
    scratch = [
        pltpu.SMEM((OFFSETS + 5,), jnp.int32),
        pltpu.SMEM((OFFSETS + 5,), jnp.int32),
        pltpu.SMEM((3, OFFSETS + 5), F32),
        pltpu.VMEM((3, SLOTS, SLOTS), F32),
        pltpu.VMEM((cells + 1, SLOTS, SLOTS), F32),
        pltpu.VMEM((cells, 8, SLOTS), F32),
        pltpu.VMEM((cells, CHANNELS, SLOTS), BF16),
        pltpu.VMEM((PAIRS, QUAD, LANES), BF16),
        pltpu.VMEM((PAIRS + 1, WIDE, LANES), BF16),
        pltpu.VMEM((PAIRS, SLOTS, LANES), F32),
        pltpu.VMEM((PAIRS, SLOTS, LANES), F32),
        pltpu.VMEM((PAIRS, SLOTS, LANES), F32),
        pltpu.VMEM((QUAD, WIDE), F32),
        pltpu.VMEM((QUAD, WIDE), F32),
        pltpu.VMEM((WIDE, LANES), F32),
        pltpu.VMEM((SLOTS, D), F32),
        pltpu.VMEM((QUAD, LANES), BF16),
        pltpu.VMEM((WIDE, LANES), BF16),
        pltpu.VMEM((QUAD, WIDE), BF16),
        pltpu.VMEM((WIDE, QUAD), BF16),
        pltpu.VMEM((3, SLOTS, SLOTS), F32),
        pltpu.VMEM((cells, CHANNELS, SLOTS), F32),
        pltpu.VMEM((cells, 8, SLOTS), F32),
    ]
    results = pl.pallas_call(
        lambda *refs: main_kernel((nxu, nyu, nzu, sizes), *refs),
        out_shape=out_shape,
        in_specs=[SMEM] + [VMEM] * (nxu + 8),
        out_specs=[VMEM] * len(out_shape),
        scratch_shapes=scratch,
        compiler_params=pltpu.CompilerParams(vmem_limit_bytes=24 << 20),
        name="pairs",
    )(
        pair_list, *blocks, feats, radial, pair_scale, w_hidden, w_zero, w_one, w_out.reshape(1, D), swap
    )
    energy, direct, keep = results[:3]
    total = keep
    for got in returned(results[3:], "gy"):
        total = total + got.astype(F32)
    sends = [total[uz * nxu : (uz + 1) * nxu].astype(BF16) for uz in range(1, nzu)]
    total = total[:nxu]
    for got in returned(sends, "gz"):
        total = total + got.astype(F32)
    sends = [total[ux : ux + 1].astype(BF16) for ux in range(1, nxu)]
    keep = total[:1]
    arrived = returned(sends, "gx")
    forces, feat_grad = pl.pallas_call(
        lambda *refs: finish_kernel(len(arrived), *refs),
        out_shape=[
            jax.ShapeDtypeStruct((1, 1, 3, 1, SLOTS), F32),
            jax.ShapeDtypeStruct((1, 1, 1, SLOTS, D), BF16),
        ],
        in_specs=[VMEM] * (3 + len(arrived)),
        out_specs=[VMEM] * 2,
        compiler_params=SMALL,
        name="finish",
    )(keep, *arrived, direct, w_env.T)
    return energy, forces.transpose(0, 1, 3, 2, 4), feat_grad


def solution(mesh):
    cell = P("gx", "gy", "gz")
    in_specs = (cell,) * 5 + (P(),) * 7
    return jax.shard_map(
        layer, mesh=mesh, in_specs=in_specs, out_specs=(cell,) * 3, check_vma=False
    )
```

```python
import jax
import jax.numpy as jnp
from jax import lax
from jax.experimental import pallas as pl
from jax.experimental.pallas import tpu as pltpu
from jax.sharding import PartitionSpec as P


D = 256
CHANNELS = 64
NBASIS = 4
NSPEC = 6
SLOTS = 128
CUTOFF = 0.55
CENTRE = 0.5
ROWS = 80
POS_ROW = 64
EXTRA_ROW = 74
LIST_LANE = 32
OFFSETS = 27
CHUNK = 16
CHUNKS = SLOTS // CHUNK
QUAD = NBASIS * SLOTS
WIDE = 4 * CHANNELS
LANES = 2 * SLOTS
NEAR_PAIRS = 5
FAR_PAIRS = 9
TOP = 8.0 * 1.4426950408889634
KAPPA = TOP**0.5
SLOPE = 4.0 * 1.4426950408889634**0.5 / TOP
SHIFT = 0.5 * 1.4426950408889634**0.5
LADDER = (1.0, 0.1353352832366127, 0.0024787521766663585, 6.14421235332821e-06)
F32 = jnp.float32
BF16 = jnp.bfloat16


def dot_nn(a, b):
    return lax.dot_general(a, b, (((1,), (0,)), ((), ())), preferred_element_type=F32)


def dot_nt(a, b):
    return lax.dot_general(a, b, (((1,), (1,)), ((), ())), preferred_element_type=F32)


def split3(value):
    high = value.astype(BF16)
    rest = value - high.astype(F32)
    middle = rest.astype(BF16)
    low = (rest - middle.astype(F32)).astype(BF16)
    return high, middle, low


def pack_kernel(
    counts_ref, feats_ref, pos_ref, species_ref, w_env_ref, list_ref, scale_ref, msg_ref, extra
):
    chans = dot_nt(w_env_ref[...], feats_ref[0, 0, 0])
    msg_ref[0, :CHANNELS] = chans.astype(BF16)
    pos = jnp.concatenate([pos_ref[0, 0, axis] for axis in range(3)], axis=0)
    slots = lax.broadcasted_iota(jnp.int32, (1, SLOTS), 1)
    counts = jnp.broadcast_to(counts_ref[0], (1, SLOTS))
    code = jnp.where(slots < counts, species_ref[0, 0].astype(F32), -1.0)
    high = pos.astype(BF16).astype(F32)
    middle = (pos - high).astype(BF16).astype(F32)
    low = pos - high - middle
    extra[...] = jnp.zeros_like(extra)
    for piece, value in enumerate(split3(scale_ref[...])):
        extra[:NSPEC, 8 * piece : 8 * piece + NSPEC] = value.astype(F32)
    extra[:1, LIST_LANE : LIST_LANE + OFFSETS] = list_ref[0, 0].astype(F32)
    tail = jnp.concatenate([high, middle, low, code, extra[:NSPEC]], axis=0)
    msg_ref[0, CHANNELS:] = tail.astype(BF16)


def row_sums(value):
    ones = jnp.ones((8, value.shape[1]), BF16)
    high, middle, low = split3(value)
    total = dot_nt(ones, high) + dot_nt(ones, middle) + dot_nt(ones, low)
    return total[0:1]


def unique_of(offset, count):
    if offset == 0 or count == 2:
        return abs(offset)
    return 1 if offset > 0 else 2


def tabulate(listed, tables, zone, sizes, counts):
    cell_of, slot_of, shift_of = tables
    nxu, nyu, nzu = counts
    live = jnp.int32(0)
    for tile in range(OFFSETS):
        offset = (tile // 9 - 1, tile // 3 % 3 - 1, tile % 3 - 1)
        if (offset[0] != 0) != zone:
            continue
        ux, uy, uz = [unique_of(o, size) for o, size in zip(offset, sizes)]
        cell = (max(ux - 1, 0) * nzu + uz) * nyu + uy
        cell_of[live] = jnp.int32(cell)
        slot_of[live] = jnp.int32(cell)
        for axis in range(3):
            shift_of[axis, live] = jnp.float32(offset[axis] * KAPPA / CUTOFF)
        live = live + listed(tile)
    for spare in (live, live + 1):
        cell_of[spare] = jnp.int32(0)
        slot_of[spare] = jnp.int32((nxu - 1 if zone else 1) * nyu * nzu)
        for axis in range(3):
            shift_of[axis, spare] = jnp.float32(0.0)
    return (live + 1) // 2


def unpack(msg_refs, counts, xj, chan):
    nyu, nzu = counts[1:]
    codes = []
    for cell in range(xj.shape[0]):
        msg = msg_refs[cell // (nyu * nzu) * nyu + cell % nyu]
        at = cell // nyu % nzu * ROWS
        tail = msg[0, at + CHANNELS : at + ROWS].astype(F32)
        place = tail[0:3] + tail[3:6] + tail[6:9]
        xj[cell, 0:3] = (place - CENTRE) * (KAPPA / CUTOFF)
        codes.append(tail[9:10])
        chan[cell] = msg[0, at : at + CHANNELS]
    return codes


def strengths(codes, onehot, scale, weight):
    scale = scale * (1.0 / (TOP * TOP))
    scale = jnp.concatenate([scale, jnp.zeros((8 - NSPEC, NSPEC), F32)], axis=0)
    coef = []
    for code in codes:
        total = jnp.zeros((8, SLOTS), F32)
        for kind in range(NSPEC):
            column = jnp.broadcast_to(scale[:, kind : kind + 1], (8, SLOTS))
            total = total + jnp.where(code == float(kind), column, 0.0)
        high = total.astype(BF16).astype(F32)
        middle = (total - high).astype(BF16).astype(F32)
        low = total - high - middle
        coef.append(
            jnp.concatenate([high, middle, low, jnp.zeros((104, SLOTS), F32)], axis=0).astype(BF16)
        )
    for cell in range(0, len(codes), 2):
        strength = dot_nn(onehot, jnp.concatenate(coef[cell : cell + 2], axis=1))
        weight[cell] = strength[:, :SLOTS]
        if cell + 1 < len(codes):
            weight[cell + 1] = strength[:, SLOTS:]
    weight[len(codes)] = jnp.zeros((SLOTS, SLOTS), F32)


def rows_of(pair, tables, xj):
    cell_of, slot_of, shift_of = tables
    first, second = 2 * pair, 2 * pair + 1
    cell_a, cell_b = cell_of[first], cell_of[second]
    rows = [
        jnp.concatenate(
            [
                xj[cell_a, axis : axis + 1] + shift_of[axis, first],
                xj[cell_b, axis : axis + 1] + shift_of[axis, second],
            ],
            axis=1,
        )
        for axis in range(3)
    ]
    return cell_a, cell_b, slot_of[first], slot_of[second], rows


def relative(rows, xi, block):
    out = []
    for axis in range(3):
        own = xi[axis, block * CHUNK : (block + 1) * CHUNK]
        out.append(rows[axis] - jnp.concatenate([own, own], axis=1))
    return out


def forward_tiles(trips, tables, xi, xj, chan, weight, saved, acc, tile_now, rmat_now):
    tiles, rmat, s_all, r_all, wb_all = saved
    tile_now[...] = jnp.zeros_like(tile_now)
    rmat_now[...] = jnp.zeros_like(rmat_now)

    def forward(pair, carry):
        acc[...] += dot_nt(tile_now[...], rmat_now[...])
        cell_a, cell_b, weight_a, weight_b, rows = rows_of(pair, tables, xj)
        for block in range(CHUNKS):
            at = slice(block * CHUNK, (block + 1) * CHUNK)
            dx, dy, dz = relative(rows, xi, block)
            s = jnp.minimum(dx * dx + dy * dy + dz * dz, TOP)
            inside = TOP - s
            spread = SLOPE * s - SHIFT
            ratio = jnp.exp2(s)
            strength = jnp.concatenate([weight[weight_a, at], weight[weight_b, at]], axis=1)
            wb = strength * jnp.exp2(-(spread * spread))
            s_all[pair, at] = s
            r_all[pair, at] = ratio
            wb_all[pair, at] = wb
            tile = wb * (inside * inside)
            for k in range(NBASIS):
                base = block * 4 * CHUNK + k * CHUNK
                rounded = tile.astype(BF16)
                tiles[pair, base : base + CHUNK] = rounded
                tile_now[base : base + CHUNK] = rounded
                if k + 1 < NBASIS:
                    tile = tile * ratio
        values = jnp.concatenate([chan[cell_a], chan[cell_b]], axis=1)
        rmat[pair, :CHANNELS] = values
        rmat_now[:CHANNELS] = values
        wide = values.astype(F32)
        for axis in range(3):
            base = (axis + 1) * CHANNELS
            scaled = (wide * rows[axis]).astype(BF16)
            rmat[pair, base : base + CHANNELS] = scaled
            rmat_now[base : base + CHANNELS] = scaled
        return carry

    lax.fori_loop(0, trips, forward, 0)
    acc[...] += dot_nt(tile_now[...], rmat_now[...])


def backward_tiles(trips, tables, xi, xj, saved, grad, gradt, pbuf, bbuf, fi, cg, pg):
    tiles, rmat, s_all, r_all, wb_all = saved
    pbuf[...] = dot_nn(grad[...], rmat[0])
    bbuf[...] = jnp.zeros_like(bbuf)
    cg[...] = jnp.zeros_like(cg)
    pg[...] = jnp.zeros_like(pg)

    def settle(pair):
        cell_a, cell_b, _, _, rows = rows_of(pair, tables, xj)
        along = [jnp.zeros((CHUNK, LANES), F32) for _ in range(3)]
        for part in range(CHANNELS // CHUNK):
            at = slice(part * CHUNK, (part + 1) * CHUNK)
            values = rmat[pair, at].astype(F32)
            sums = bbuf[part * 4 * CHUNK : part * 4 * CHUNK + CHUNK]
            for axis in range(3):
                base = part * 4 * CHUNK + (axis + 1) * CHUNK
                piece = bbuf[base : base + CHUNK]
                sums = sums + rows[axis] * piece
                along[axis] = along[axis] + values * piece
            cg[cell_a, at] += sums[:, :SLOTS]
            cg[cell_b, at] += sums[:, SLOTS:]
        for axis in range(3):
            total = KAPPA * jnp.sum(along[axis], axis=0, keepdims=True)
            pg[cell_a, axis : axis + 1] += total[:, :SLOTS]
            pg[cell_b, axis : axis + 1] += total[:, SLOTS:]

    def backward(pair, carry):
        cell_a, cell_b, _, _, rows = rows_of(pair, tables, xj)
        totals = [jnp.zeros((CHUNK, LANES), F32) for _ in range(3)]
        for block in range(CHUNKS):
            at = slice(block * CHUNK, (block + 1) * CHUNK)
            s = s_all[pair, at]
            ratio = r_all[pair, at]
            inside = TOP - s
            step = 8.0 * inside
            level = -2.0 * TOP - inside * ((32.0 / TOP) * s - 4.0)
            levels = [level]
            for _ in range(1, NBASIS):
                levels.append(levels[-1] + step)
            base = block * 4 * CHUNK
            slope = levels[3] * pbuf[base + 3 * CHUNK : base + 4 * CHUNK]
            for k in (2, 1, 0):
                slope = slope * ratio + levels[k] * pbuf[base + k * CHUNK : base + (k + 1) * CHUNK]
            slope = slope * (wb_all[pair, at] * inside)
            for axis, delta in enumerate(relative(rows, xi, block)):
                push = slope * delta
                totals[axis] = totals[axis] + push
                fi[axis, at] += push[:, :SLOTS] + push[:, SLOTS:]
        for axis in range(3):
            total = (2.0 / KAPPA) * jnp.sum(totals[axis], axis=0, keepdims=True)
            pg[cell_a, axis : axis + 1] += total[:, :SLOTS]
            pg[cell_b, axis : axis + 1] += total[:, SLOTS:]
        settle(jnp.maximum(pair - 1, 0))
        pbuf[...] = dot_nn(grad[...], rmat[pair + 1])
        bbuf[...] = dot_nn(gradt[...], tiles[pair])
        return carry

    lax.fori_loop(0, trips, backward, 0)

    @pl.when(trips > 0)
    def _():
        settle(trips - 1)


def write_out(out_refs, counts, cg, pg, slots):
    nyu, nzu = counts[1:]
    for cell in range(cg.shape[0]):
        out = out_refs[cell % nyu]
        at = slots[cell // (nyu * nzu)] * nzu + cell // nyu % nzu
        out[at, :CHANNELS] = cg[cell].astype(out.dtype)
        tail = jnp.concatenate([pg[cell], jnp.zeros((8, SLOTS), F32)], axis=0)
        out[at, CHANNELS:] = (tail * (1.0 / CUTOFF)).astype(out.dtype)


def inner_kernel(sizes, counts, *refs):
    _, nyu, _ = counts
    msg_refs = refs[:nyu]
    xi, code_ref, onehot_ref, xj, acc, *saved = refs[nyu : 10 + nyu]
    (
        cell_of, slot_of, shift_of, weight, chan, tile_now, rmat_now, list_row, list_ref, sem,
    ) = refs[10 + nyu :]
    tables = (cell_of, slot_of, shift_of)
    tail = msg_refs[0][0, CHANNELS:ROWS].astype(F32)
    extra = tail[EXTRA_ROW - CHANNELS : EXTRA_ROW - CHANNELS + NSPEC]
    list_row[...] = extra[:1].astype(jnp.int32)
    list_copy = pltpu.make_async_copy(list_row, list_ref, sem)
    list_copy.start()
    scale = extra[:, :NSPEC] + extra[:, 8 : 8 + NSPEC] + extra[:, 16 : 16 + NSPEC]
    codes = unpack(msg_refs, counts, xj, chan)
    for axis in range(3):
        xi[axis] = jnp.broadcast_to(xj[0, axis : axis + 1], (SLOTS, SLOTS)).T
    code_i = jnp.broadcast_to(codes[0], (SLOTS, SLOTS)).T
    code_ref[...] = code_i
    lane = lax.broadcasted_iota(jnp.int32, (SLOTS, SLOTS), 1)
    sub = lax.broadcasted_iota(jnp.int32, (SLOTS, SLOTS), 0)
    onehot = jnp.where((code_i == (lane % 8).astype(F32)) & (lane < 24), 1.0, 0.0)
    onehot = onehot.astype(BF16)
    onehot_ref[...] = onehot
    strengths(codes, onehot, scale, weight)
    list_copy.wait()
    trips = tabulate(lambda tile: list_ref[0, LIST_LANE + tile], tables, False, sizes, counts)
    weight[0] = jnp.where(lane == sub, 0.0, weight[0])
    acc[...] = jnp.zeros_like(acc)
    forward_tiles(trips, tables, xi, xj, chan, weight, saved, acc, tile_now, rmat_now)


def outer_kernel(sizes, counts, *refs):
    nxu, nyu, _ = counts
    far = (nxu - 1) * nyu
    list_ref, msg_refs = refs[0], refs[1 : 1 + far]
    refs = refs[1 + far :]
    scale_ref, radial_ref, w_zero_ref, w_one_ref, w_out_ref, swap_ref = refs[:6]
    feats_ref, w_hidden_ref, xi, code_ref, onehot_ref, acc_in = refs[6:12]
    grad, gradt, fi, pre_ref, heat_ref = refs[12:17]
    out_refs = refs[17 : 17 + nyu]
    (
        cell_of, slot_of, shift_of, weight, xj, chan, tiles, rmat, s_all, r_all, wb_all,
        acc, pbuf, bbuf, tile_now, rmat_now, cg, pg, hbuf,
    ) = refs[17 + nyu :]
    tables = (cell_of, slot_of, shift_of)
    saved = (tiles, rmat, s_all, r_all, wb_all)
    trips = tabulate(lambda tile: list_ref[0, 0, 0, tile], tables, True, sizes, counts)
    codes = unpack(msg_refs, counts, xj, chan)
    strengths(codes, onehot_ref[...], scale_ref[...], weight)
    acc[...] = acc_in[...]
    hbuf[...] = dot_nn(feats_ref[0, 0, 0], w_hidden_ref[...])
    forward_tiles(trips, tables, xi, xj, chan, weight, saved, acc, tile_now, rmat_now)

    radial = radial_ref[...]
    weights_k = []
    for k in range(NBASIS):
        row = radial[k : k + 1] * LADDER[k]
        weights_k.append(jnp.concatenate([row] + [row * (1.0 / KAPPA)] * 3, axis=1))
    mixed = []
    for block in range(CHUNKS):
        base = block * 4 * CHUNK
        total = weights_k[0] * acc[base : base + CHUNK]
        for k in range(1, NBASIS):
            total = total + weights_k[k] * acc[base + k * CHUNK : base + (k + 1) * CHUNK]
        mixed.append(total)
    mixed = jnp.concatenate(mixed, axis=0)
    low = lax.broadcasted_iota(jnp.int32, (SLOTS, SLOTS), 1) < CHANNELS
    left, right = mixed[:, :SLOTS], mixed[:, SLOTS:]
    scalar = jnp.where(low, left, pltpu.roll(left, CHANNELS, 1))
    own_left = jnp.where(low, 0.0, xi[0]) * (1.0 / KAPPA)
    own_right = jnp.where(low, xi[1], xi[2]) * (1.0 / KAPPA)
    left = left - own_left * scalar
    right = right - own_right * scalar
    features = [jnp.where(low, left, left * left), right * right]
    features = jnp.concatenate(features, axis=1).astype(BF16)
    w_one = w_one_ref[...]
    w_all = jnp.concatenate([w_zero_ref[...], w_one, w_one, w_one], axis=0)
    pre = hbuf[...] + dot_nn(features, w_all)
    gate = jax.nn.sigmoid(pre)
    occupied = jnp.concatenate([code_ref[...], code_ref[...]], axis=1) >= 0.0
    w_out = jnp.where(occupied, w_out_ref[...], 0.0)
    pre_grad = (w_out * gate * (1.0 + pre * (1.0 - gate))).astype(BF16)
    back_all = dot_nt(pre_grad, w_all)
    back_left, back_right = back_all[:, :SLOTS], back_all[:, SLOTS:]
    part_left = jnp.where(low, back_left, 2.0 * left * back_left)
    part_right = 2.0 * right * back_right
    fold = own_left * part_left + own_right * part_right
    fold = fold + pltpu.roll(fold, CHANNELS, 1)
    full = jnp.concatenate([part_left - jnp.where(low, fold, 0.0), part_right], axis=1)
    half = (0.5 * KAPPA) * scalar
    fi[0] = jnp.where(low, 0.0, half * part_left)
    fi[1] = jnp.where(low, half * part_right, 0.0)
    fi[2] = jnp.where(low, 0.0, half * part_right)
    for block in range(CHUNKS):
        piece = full[block * CHUNK : (block + 1) * CHUNK]
        for k in range(NBASIS):
            base = block * 4 * CHUNK + k * CHUNK
            scaled = weights_k[k] * piece
            grad[base : base + CHUNK] = scaled.astype(BF16)
    gradt[...] = dot_nt(swap_ref[...], grad[...]).astype(BF16)
    pre_ref[...] = pre_grad
    heat_ref[...] = pre * gate * w_out
    backward_tiles(trips, tables, xi, xj, saved, grad, gradt, pbuf, bbuf, fi, cg, pg)
    slots = [0, 1]
    if sizes[0] > 2 and sizes[0] % 2 == 0:
        odd = lax.rem(lax.axis_index("gx"), 2)
        slots = [1 - odd, odd]
    write_out(out_refs, counts, cg, pg, slots)


def rest_kernel(sizes, counts, *refs):
    nyu = counts[1]
    list_ref, w_hidden_ref, xi, xj, *saved = refs[:9]
    grad, gradt, fi_in, pre_ref, heat_ref = refs[9:14]
    energy_ref, direct_ref = refs[14:16]
    out_refs = refs[16 : 16 + nyu]
    cell_of, slot_of, shift_of, pbuf, bbuf, fi, cg, pg = refs[16 + nyu :]
    tables = (cell_of, slot_of, shift_of)
    trips = tabulate(lambda tile: list_ref[0, 0, 0, tile], tables, False, sizes, counts)
    energy_ref[0, 0] = row_sums(heat_ref[...])
    direct_ref[...] = dot_nt(pre_ref[...], w_hidden_ref[...])
    fi[...] = fi_in[...]
    backward_tiles(trips, tables, xi, xj, saved, grad, gradt, pbuf, bbuf, fi, cg, pg)
    for axis in range(3):
        pg[0, axis : axis + 1] -= (2.0 / KAPPA) * row_sums(fi[axis])
    write_out(out_refs, counts, cg, pg, [0])


def finish_kernel(count, *refs):
    keep_ref = refs[0]
    got_refs = refs[1 : 1 + count]
    direct_ref, w_env_ref, force_ref, grad_ref = refs[1 + count :]
    total = keep_ref[0]
    for got in got_refs:
        total = total + got[0].astype(F32)
    chan = total[:CHANNELS]
    high = chan.astype(BF16)
    low = (chan - high.astype(F32)).astype(BF16)
    both = jnp.concatenate([high, low], axis=0)
    w_env = w_env_ref[...]
    weights = jnp.concatenate([w_env, w_env], axis=0)
    part = lax.dot_general(both, weights, (((0,), (0,)), ((), ())), preferred_element_type=F32)
    grad_ref[0, 0, 0] = (direct_ref[...] + part).astype(BF16)
    for axis in range(3):
        force_ref[0, 0, axis] = -total[POS_ROW + axis : POS_ROW + axis + 1]


def shifted(value, axis, steps):
    count = lax.axis_size(axis)
    return lax.ppermute(value, axis, [(i, (i + steps) % count) for i in range(count)])


def gathered(value, axis):
    if lax.axis_size(axis) == 2:
        return [value, shifted(value, axis, 1)]
    up = shifted(value, axis, -1)
    down = shifted(value, axis, 1)
    return [value, up, down]


def returned(parts, axis):
    count = lax.axis_size(axis)
    if count == 2:
        return [shifted(parts[0], axis, 1)]
    return [shifted(parts[1], axis, -1), shifted(parts[0], axis, 1)]


def swapped(parts, axis):
    count = lax.axis_size(axis)
    if count == 2 or count % 2:
        return returned(parts, axis)
    ring = [(i, ((((i + 1) % count) ^ 1) - 1) % count) for i in range(count)]
    far = lax.ppermute(parts[0], axis, ring)
    near = lax.ppermute(parts[1], axis, [(i, i ^ 1) for i in range(count)])
    return [far, near]


VMEM = pl.BlockSpec(memory_space=pltpu.VMEM)
SMEM = pl.BlockSpec(memory_space=pltpu.SMEM)
SMALL = pltpu.CompilerParams(vmem_limit_bytes=4 << 20)


def layer(
    feats, positions, species, cell_counts, pair_list, w_env, radial, pair_scale, w_hidden,
    w_zero, w_one, w_out,
):
    sizes = [lax.axis_size(axis) for axis in ("gx", "gy", "gz")]
    nxu, nyu, nzu = [2 if size == 2 else 3 for size in sizes]
    msg = pl.pallas_call(
        pack_kernel,
        out_shape=jax.ShapeDtypeStruct((1, ROWS, SLOTS), BF16),
        in_specs=[VMEM] * 7,
        out_specs=VMEM,
        scratch_shapes=[pltpu.VMEM((8, SLOTS), F32)],
        name="pack",
    )(
        cell_counts, feats, positions.transpose(0, 1, 3, 2, 4), species, w_env.T, pair_list,
        pair_scale,
    )
    stack = gathered(msg, "gz")
    column = jnp.pad(msg, ((0, 0), (0, ROWS * (nzu - 1)), (0, 0)))
    column = lax.optimization_barrier(column)
    for uz in range(1, nzu):
        column = lax.dynamic_update_slice(column, stack[uz], (0, uz * ROWS, 0))
    blocks = [gathered(part, "gy") for part in gathered(column, "gx")]
    near_blocks = blocks[0]
    far_blocks = [block for part in blocks[1:] for block in part]
    counts = (nxu, nyu, nzu)
    near_cells, far_cells = nyu * nzu, (nxu - 1) * nyu * nzu

    def table_scratch():
        return [
            pltpu.SMEM((OFFSETS + 5,), jnp.int32),
            pltpu.SMEM((OFFSETS + 5,), jnp.int32),
            pltpu.SMEM((3, OFFSETS + 5), F32),
        ]

    def saved_shapes(pairs):
        return [
            ((pairs, QUAD, LANES), BF16),
            ((pairs + 1, WIDE, LANES), BF16),
            ((pairs, SLOTS, LANES), F32),
            ((pairs, SLOTS, LANES), F32),
            ((pairs, SLOTS, LANES), F32),
        ]

    square = (SLOTS, SLOTS)
    now_scratch = [pltpu.VMEM((QUAD, LANES), BF16), pltpu.VMEM((WIDE, LANES), BF16)]
    buffers = [pltpu.VMEM((QUAD, WIDE), F32), pltpu.VMEM((WIDE, LANES), F32)]

    def sums_scratch(cells):
        return [pltpu.VMEM((cells, CHANNELS, SLOTS), F32), pltpu.VMEM((cells, 8, SLOTS), F32)]

    def call(kernel, shapes, scratch, megabytes, first, *operands):
        return pl.pallas_call(
            lambda *refs: kernel(sizes, counts, *refs),
            out_shape=[jax.ShapeDtypeStruct(*shape) for shape in shapes],
            in_specs=first + [VMEM] * (len(operands) - len(first)),
            out_specs=[VMEM] * len(shapes),
            scratch_shapes=scratch,
            compiler_params=pltpu.CompilerParams(vmem_limit_bytes=megabytes << 20),
            cost_estimate=pl.CostEstimate(
                flops=1000000000, bytes_accessed=4000000, transcendentals=0
            ),
        )(*operands)

    inner = call(
        inner_kernel,
        [
            ((3,) + square, F32),
            (square, F32),
            (square, BF16),
            ((near_cells, 8, SLOTS), F32),
            ((QUAD, WIDE), F32),
        ]
        + saved_shapes(NEAR_PAIRS),
        table_scratch()
        + [pltpu.VMEM((near_cells + 1,) + square, F32)]
        + [pltpu.VMEM((near_cells, CHANNELS, SLOTS), BF16)]
        + now_scratch
        + [
            pltpu.VMEM((1, SLOTS), jnp.int32),
            pltpu.SMEM((1, SLOTS), jnp.int32),
            pltpu.SemaphoreType.DMA,
        ],
        12,
        [],
        *near_blocks,
    )
    xi, code, onehot, xj, acc = inner[:5]
    saved = inner[5:]
    place = jnp.arange(WIDE)
    held = place % CHUNK + place // (4 * CHUNK) * CHUNK + place // CHUNK % 4 * CHANNELS
    swap = (held[:, None] == place[None, :]).astype(BF16)
    far_out = (nxu - 1) * nzu
    outer = call(
        outer_kernel,
        [
            ((QUAD, WIDE), BF16),
            ((WIDE, QUAD), BF16),
            ((3,) + square, F32),
            ((SLOTS, D), BF16),
            ((SLOTS, D), F32),
            ((far_out, ROWS, SLOTS), F32),
        ]
        + [((far_out, ROWS, SLOTS), BF16)] * (nyu - 1),
        table_scratch()
        + [pltpu.VMEM((far_cells + 1,) + square, F32)]
        + [pltpu.VMEM((far_cells, 8, SLOTS), F32)]
        + [pltpu.VMEM((far_cells, CHANNELS, SLOTS), BF16)]
        + [pltpu.VMEM(*shape) for shape in saved_shapes(FAR_PAIRS)]
        + [pltpu.VMEM((QUAD, WIDE), F32)]
        + buffers
        + now_scratch
        + sums_scratch(far_cells)
        + [pltpu.VMEM((SLOTS, D), F32)],
        20,
        [SMEM],
        pair_list, *far_blocks, pair_scale, radial, w_zero, w_one, w_out.reshape(1, D), swap,
        feats, w_hidden, xi, code, onehot, acc,
    )
    grad, gradt, force_in, pre_grad, heat = outer[:5]
    total = outer[5]
    for got in returned(outer[6:], "gy"):
        total = total + got.astype(F32)
    sends = [total[ux * nzu : (ux + 1) * nzu].astype(BF16) for ux in range(nxu - 1)]
    from_far = swapped(sends, "gx")
    rest = call(
        rest_kernel,
        [((1, 1, 1, SLOTS), F32), ((SLOTS, D), F32), ((nzu, ROWS, SLOTS), F32)]
        + [((nzu, ROWS, SLOTS), BF16)] * (nyu - 1),
        table_scratch()
        + buffers
        + [pltpu.VMEM((3,) + square, F32)]
        + sums_scratch(near_cells),
        12,
        [SMEM],
        pair_list, w_hidden, xi, xj, *saved, grad, gradt, force_in, pre_grad, heat,
    )
    energy, direct, total = rest[:3]
    for got in returned(rest[3:], "gy"):
        total = total + got.astype(F32)
    for got in from_far:
        total = total + got.astype(F32)
    sends = [total[uz : uz + 1].astype(BF16) for uz in range(1, nzu)]
    keep = total[:1]
    arrived = returned(sends, "gz")
    forces, feat_grad = pl.pallas_call(
        lambda *refs: finish_kernel(len(arrived), *refs),
        out_shape=[
            jax.ShapeDtypeStruct((1, 1, 3, 1, SLOTS), F32),
            jax.ShapeDtypeStruct((1, 1, 1, SLOTS, D), BF16),
        ],
        in_specs=[VMEM] * (3 + len(arrived)),
        out_specs=[VMEM] * 2,
        compiler_params=SMALL,
        name="finish",
    )(keep, *arrived, direct, w_env.T)
    return energy, forces.transpose(0, 1, 3, 2, 4), feat_grad


def solution(mesh):
    cell = P("gx", "gy", "gz")
    in_specs = (cell,) * 5 + (P(),) * 7
    return jax.shard_map(
        layer, mesh=mesh, in_specs=in_specs, out_specs=(cell,) * 3, check_vma=False
    )
```

```python
import jax
import jax.numpy as jnp
from jax import lax
from jax.experimental import pallas as pl
from jax.experimental.pallas import tpu as pltpu
from jax.sharding import PartitionSpec as P


D = 256
CHANNELS = 64
NBASIS = 4
NSPEC = 6
SLOTS = 128
CUTOFF = 0.55
CENTRE = 0.5
ROWS = 80
POS_ROW = 64
EXTRA_ROW = 74
LIST_LANE = 32
OFFSETS = 27
CHUNK = 16
CHUNKS = SLOTS // CHUNK
QUAD = NBASIS * SLOTS
WIDE = 4 * CHANNELS
LANES = 2 * SLOTS
NEAR_PAIRS = 5
FAR_PAIRS = 9
TOP = 8.0 * 1.4426950408889634
KAPPA = TOP**0.5
SLOPE = 4.0 * 1.4426950408889634**0.5 / TOP
SHIFT = 0.5 * 1.4426950408889634**0.5
LADDER = (1.0, 0.1353352832366127, 0.0024787521766663585, 6.14421235332821e-06)
F32 = jnp.float32
BF16 = jnp.bfloat16


def dot_nn(a, b):
    return lax.dot_general(a, b, (((1,), (0,)), ((), ())), preferred_element_type=F32)


def dot_nt(a, b):
    return lax.dot_general(a, b, (((1,), (1,)), ((), ())), preferred_element_type=F32)


def split3(value):
    high = value.astype(BF16)
    rest = value - high.astype(F32)
    middle = rest.astype(BF16)
    low = (rest - middle.astype(F32)).astype(BF16)
    return high, middle, low


def pack_kernel(
    counts_ref, feats_ref, pos_ref, species_ref, w_env_ref, list_ref, scale_ref, msg_ref, extra
):
    chans = dot_nt(w_env_ref[...], feats_ref[0, 0, 0])
    msg_ref[0, :CHANNELS] = chans.astype(BF16)
    pos = jnp.concatenate([pos_ref[0, 0, axis] for axis in range(3)], axis=0)
    slots = lax.broadcasted_iota(jnp.int32, (1, SLOTS), 1)
    counts = jnp.broadcast_to(counts_ref[0], (1, SLOTS))
    code = jnp.where(slots < counts, species_ref[0, 0].astype(F32), -1.0)
    high = pos.astype(BF16).astype(F32)
    middle = (pos - high).astype(BF16).astype(F32)
    low = pos - high - middle
    extra[...] = jnp.zeros_like(extra)
    for piece, value in enumerate(split3(scale_ref[...])):
        extra[:NSPEC, 8 * piece : 8 * piece + NSPEC] = value.astype(F32)
    extra[:1, LIST_LANE : LIST_LANE + OFFSETS] = list_ref[0, 0].astype(F32)
    tail = jnp.concatenate([high, middle, low, code, extra[:NSPEC]], axis=0)
    msg_ref[0, CHANNELS:] = tail.astype(BF16)


def row_sums(value):
    ones = jnp.ones((8, value.shape[1]), BF16)
    high, middle, low = split3(value)
    total = dot_nt(ones, high) + dot_nt(ones, middle) + dot_nt(ones, low)
    return total[0:1]


def unique_of(offset, count):
    if offset == 0 or count == 2:
        return abs(offset)
    return 1 if offset > 0 else 2


def tabulate(listed, tables, zone, sizes, counts):
    cell_of, slot_of, shift_of = tables
    nxu, nyu, nzu = counts
    live = jnp.int32(0)
    for tile in range(OFFSETS):
        offset = (tile // 9 - 1, tile // 3 % 3 - 1, tile % 3 - 1)
        if (offset[0] != 0) != zone:
            continue
        ux, uy, uz = [unique_of(o, size) for o, size in zip(offset, sizes)]
        cell = (max(ux - 1, 0) * nzu + uz) * nyu + uy
        cell_of[live] = jnp.int32(cell)
        slot_of[live] = jnp.int32(cell)
        for axis in range(3):
            shift_of[axis, live] = jnp.float32(offset[axis] * KAPPA / CUTOFF)
        live = live + listed(tile)
    for spare in (live, live + 1):
        cell_of[spare] = jnp.int32(0)
        slot_of[spare] = jnp.int32((nxu - 1 if zone else 1) * nyu * nzu)
        for axis in range(3):
            shift_of[axis, spare] = jnp.float32(0.0)
    return (live + 1) // 2


def unpack(msg_refs, counts, xj, chan):
    nyu, nzu = counts[1:]
    codes = []
    for cell in range(xj.shape[0]):
        msg = msg_refs[cell // (nyu * nzu) * nyu + cell % nyu]
        at = cell // nyu % nzu * ROWS
        tail = msg[0, at + CHANNELS : at + ROWS].astype(F32)
        place = tail[0:3] + tail[3:6] + tail[6:9]
        xj[cell, 0:3] = (place - CENTRE) * (KAPPA / CUTOFF)
        codes.append(tail[9:10])
        chan[cell] = msg[0, at : at + CHANNELS]
    return codes


def strengths(codes, onehot, scale, weight):
    scale = scale * (1.0 / (TOP * TOP))
    scale = jnp.concatenate([scale, jnp.zeros((8 - NSPEC, NSPEC), F32)], axis=0)
    coef = []
    for code in codes:
        total = jnp.zeros((8, SLOTS), F32)
        for kind in range(NSPEC):
            column = jnp.broadcast_to(scale[:, kind : kind + 1], (8, SLOTS))
            total = total + jnp.where(code == float(kind), column, 0.0)
        high = total.astype(BF16).astype(F32)
        middle = (total - high).astype(BF16).astype(F32)
        low = total - high - middle
        coef.append(
            jnp.concatenate([high, middle, low, jnp.zeros((104, SLOTS), F32)], axis=0).astype(BF16)
        )
    for cell in range(0, len(codes), 2):
        strength = dot_nn(onehot, jnp.concatenate(coef[cell : cell + 2], axis=1))
        weight[cell] = strength[:, :SLOTS]
        if cell + 1 < len(codes):
            weight[cell + 1] = strength[:, SLOTS:]
    weight[len(codes)] = jnp.zeros((SLOTS, SLOTS), F32)


def rows_of(pair, tables, xj):
    cell_of, slot_of, shift_of = tables
    first, second = 2 * pair, 2 * pair + 1
    cell_a, cell_b = cell_of[first], cell_of[second]
    rows = [
        jnp.concatenate(
            [
                xj[cell_a, axis : axis + 1] + shift_of[axis, first],
                xj[cell_b, axis : axis + 1] + shift_of[axis, second],
            ],
            axis=1,
        )
        for axis in range(3)
    ]
    return cell_a, cell_b, slot_of[first], slot_of[second], rows


def relative(rows, xi, block):
    out = []
    for axis in range(3):
        own = xi[axis, block * CHUNK : (block + 1) * CHUNK]
        out.append(rows[axis] - jnp.concatenate([own, own], axis=1))
    return out


def forward_tiles(trips, tables, xi, xj, chan, weight, saved, acc, tile_now, rmat_now):
    tiles, rmat, s_all, r_all, wb_all = saved
    tile_now[...] = jnp.zeros_like(tile_now)
    rmat_now[...] = jnp.zeros_like(rmat_now)

    def forward(pair, carry):
        acc[...] += dot_nt(tile_now[...], rmat_now[...])
        cell_a, cell_b, weight_a, weight_b, rows = rows_of(pair, tables, xj)
        for block in range(CHUNKS):
            at = slice(block * CHUNK, (block + 1) * CHUNK)
            dx, dy, dz = relative(rows, xi, block)
            s = jnp.minimum(dx * dx + dy * dy + dz * dz, TOP)
            inside = TOP - s
            spread = SLOPE * s - SHIFT
            ratio = jnp.exp2(s)
            strength = jnp.concatenate([weight[weight_a, at], weight[weight_b, at]], axis=1)
            wb = strength * jnp.exp2(-(spread * spread))
            s_all[pair, at] = s
            r_all[pair, at] = ratio
            wb_all[pair, at] = wb
            tile = wb * (inside * inside)
            for k in range(NBASIS):
                base = block * 4 * CHUNK + k * CHUNK
                rounded = tile.astype(BF16)
                tiles[pair, base : base + CHUNK] = rounded
                tile_now[base : base + CHUNK] = rounded
                if k + 1 < NBASIS:
                    tile = tile * ratio
        values = jnp.concatenate([chan[cell_a], chan[cell_b]], axis=1)
        rmat[pair, :CHANNELS] = values
        rmat_now[:CHANNELS] = values
        wide = values.astype(F32)
        for axis in range(3):
            base = (axis + 1) * CHANNELS
            scaled = (wide * rows[axis]).astype(BF16)
            rmat[pair, base : base + CHANNELS] = scaled
            rmat_now[base : base + CHANNELS] = scaled
        return carry

    lax.fori_loop(0, trips, forward, 0)
    acc[...] += dot_nt(tile_now[...], rmat_now[...])


def backward_tiles(trips, tables, xi, xj, saved, grad, gradt, pbuf, bbuf, fi, cg, pg):
    tiles, rmat, s_all, r_all, wb_all = saved
    pbuf[...] = dot_nn(grad[...], rmat[0])
    bbuf[...] = jnp.zeros_like(bbuf)
    cg[...] = jnp.zeros_like(cg)
    pg[...] = jnp.zeros_like(pg)

    def settle(pair):
        cell_a, cell_b, _, _, rows = rows_of(pair, tables, xj)
        along = [jnp.zeros((CHUNK, LANES), F32) for _ in range(3)]
        for part in range(CHANNELS // CHUNK):
            at = slice(part * CHUNK, (part + 1) * CHUNK)
            values = rmat[pair, at].astype(F32)
            sums = bbuf[part * 4 * CHUNK : part * 4 * CHUNK + CHUNK]
            for axis in range(3):
                base = part * 4 * CHUNK + (axis + 1) * CHUNK
                piece = bbuf[base : base + CHUNK]
                sums = sums + rows[axis] * piece
                along[axis] = along[axis] + values * piece
            cg[cell_a, at] += sums[:, :SLOTS]
            cg[cell_b, at] += sums[:, SLOTS:]
        for axis in range(3):
            total = KAPPA * jnp.sum(along[axis], axis=0, keepdims=True)
            pg[cell_a, axis : axis + 1] += total[:, :SLOTS]
            pg[cell_b, axis : axis + 1] += total[:, SLOTS:]

    def backward(pair, carry):
        cell_a, cell_b, _, _, rows = rows_of(pair, tables, xj)
        settle(jnp.maximum(pair - 1, 0))
        totals = [jnp.zeros((CHUNK, LANES), F32) for _ in range(3)]
        for block in range(CHUNKS):
            at = slice(block * CHUNK, (block + 1) * CHUNK)
            s = s_all[pair, at]
            ratio = r_all[pair, at]
            inside = TOP - s
            step = 8.0 * inside
            level = -2.0 * TOP - inside * ((32.0 / TOP) * s - 4.0)
            levels = [level]
            for _ in range(1, NBASIS):
                levels.append(levels[-1] + step)
            base = block * 4 * CHUNK
            slope = levels[3] * pbuf[base + 3 * CHUNK : base + 4 * CHUNK]
            for k in (2, 1, 0):
                slope = slope * ratio + levels[k] * pbuf[base + k * CHUNK : base + (k + 1) * CHUNK]
            slope = slope * (wb_all[pair, at] * inside)
            for axis, delta in enumerate(relative(rows, xi, block)):
                push = slope * delta
                totals[axis] = totals[axis] + push
                fi[axis, at] += push[:, :SLOTS] + push[:, SLOTS:]
        for axis in range(3):
            total = (2.0 / KAPPA) * jnp.sum(totals[axis], axis=0, keepdims=True)
            pg[cell_a, axis : axis + 1] += total[:, :SLOTS]
            pg[cell_b, axis : axis + 1] += total[:, SLOTS:]
        pbuf[...] = dot_nn(grad[...], rmat[pair + 1])
        bbuf[...] = dot_nn(gradt[...], tiles[pair])
        return carry

    lax.fori_loop(0, trips, backward, 0)

    @pl.when(trips > 0)
    def _():
        settle(trips - 1)


def write_out(out_refs, counts, cg, pg, slots):
    nyu, nzu = counts[1:]
    for cell in range(cg.shape[0]):
        out = out_refs[cell % nyu]
        at = slots[cell // (nyu * nzu)] * nzu + cell // nyu % nzu
        out[at, :CHANNELS] = cg[cell].astype(out.dtype)
        tail = jnp.concatenate([pg[cell], jnp.zeros((8, SLOTS), F32)], axis=0)
        out[at, CHANNELS:] = (tail * (1.0 / CUTOFF)).astype(out.dtype)


def inner_kernel(sizes, counts, *refs):
    _, nyu, _ = counts
    msg_refs = refs[:nyu]
    xi, code_ref, onehot_ref, xj, acc, *saved = refs[nyu : 10 + nyu]
    (
        cell_of, slot_of, shift_of, weight, chan, tile_now, rmat_now, list_row, list_ref, sem,
    ) = refs[10 + nyu :]
    tables = (cell_of, slot_of, shift_of)
    tail = msg_refs[0][0, CHANNELS:ROWS].astype(F32)
    extra = tail[EXTRA_ROW - CHANNELS : EXTRA_ROW - CHANNELS + NSPEC]
    list_row[...] = extra[:1].astype(jnp.int32)
    list_copy = pltpu.make_async_copy(list_row, list_ref, sem)
    list_copy.start()
    scale = extra[:, :NSPEC] + extra[:, 8 : 8 + NSPEC] + extra[:, 16 : 16 + NSPEC]
    codes = unpack(msg_refs, counts, xj, chan)
    for axis in range(3):
        xi[axis] = jnp.broadcast_to(xj[0, axis : axis + 1], (SLOTS, SLOTS)).T
    code_i = jnp.broadcast_to(codes[0], (SLOTS, SLOTS)).T
    code_ref[...] = code_i
    lane = lax.broadcasted_iota(jnp.int32, (SLOTS, SLOTS), 1)
    sub = lax.broadcasted_iota(jnp.int32, (SLOTS, SLOTS), 0)
    onehot = jnp.where((code_i == (lane % 8).astype(F32)) & (lane < 24), 1.0, 0.0)
    onehot = onehot.astype(BF16)
    onehot_ref[...] = onehot
    strengths(codes, onehot, scale, weight)
    list_copy.wait()
    trips = tabulate(lambda tile: list_ref[0, LIST_LANE + tile], tables, False, sizes, counts)
    weight[0] = jnp.where(lane == sub, 0.0, weight[0])
    acc[...] = jnp.zeros_like(acc)
    forward_tiles(trips, tables, xi, xj, chan, weight, saved, acc, tile_now, rmat_now)


def outer_kernel(sizes, counts, *refs):
    nxu, nyu, _ = counts
    far = (nxu - 1) * nyu
    list_ref, msg_refs = refs[0], refs[1 : 1 + far]
    refs = refs[1 + far :]
    scale_ref, radial_ref, w_zero_ref, w_one_ref, w_out_ref, swap_ref = refs[:6]
    feats_ref, w_hidden_ref, xi, code_ref, onehot_ref, acc_in = refs[6:12]
    grad, gradt, fi, pre_ref, heat_ref = refs[12:17]
    out_refs = refs[17 : 17 + nyu]
    (
        cell_of, slot_of, shift_of, weight, xj, chan, tiles, rmat, s_all, r_all, wb_all,
        acc, pbuf, bbuf, tile_now, rmat_now, cg, pg, hbuf,
    ) = refs[17 + nyu :]
    tables = (cell_of, slot_of, shift_of)
    saved = (tiles, rmat, s_all, r_all, wb_all)
    trips = tabulate(lambda tile: list_ref[0, 0, 0, tile], tables, True, sizes, counts)
    codes = unpack(msg_refs, counts, xj, chan)
    strengths(codes, onehot_ref[...], scale_ref[...], weight)
    acc[...] = acc_in[...]
    hbuf[...] = dot_nn(feats_ref[0, 0, 0], w_hidden_ref[...])
    forward_tiles(trips, tables, xi, xj, chan, weight, saved, acc, tile_now, rmat_now)

    radial = radial_ref[...]
    weights_k = []
    for k in range(NBASIS):
        row = radial[k : k + 1] * LADDER[k]
        weights_k.append(jnp.concatenate([row] + [row * (1.0 / KAPPA)] * 3, axis=1))
    mixed = []
    for block in range(CHUNKS):
        base = block * 4 * CHUNK
        total = weights_k[0] * acc[base : base + CHUNK]
        for k in range(1, NBASIS):
            total = total + weights_k[k] * acc[base + k * CHUNK : base + (k + 1) * CHUNK]
        mixed.append(total)
    mixed = jnp.concatenate(mixed, axis=0)
    low = lax.broadcasted_iota(jnp.int32, (SLOTS, SLOTS), 1) < CHANNELS
    left, right = mixed[:, :SLOTS], mixed[:, SLOTS:]
    scalar = jnp.where(low, left, pltpu.roll(left, CHANNELS, 1))
    own_left = jnp.where(low, 0.0, xi[0]) * (1.0 / KAPPA)
    own_right = jnp.where(low, xi[1], xi[2]) * (1.0 / KAPPA)
    left = left - own_left * scalar
    right = right - own_right * scalar
    features = [jnp.where(low, left, left * left), right * right]
    features = jnp.concatenate(features, axis=1).astype(BF16)
    w_one = w_one_ref[...]
    w_all = jnp.concatenate([w_zero_ref[...], w_one, w_one, w_one], axis=0)
    pre = hbuf[...] + dot_nn(features, w_all)
    gate = jax.nn.sigmoid(pre)
    occupied = jnp.concatenate([code_ref[...], code_ref[...]], axis=1) >= 0.0
    w_out = jnp.where(occupied, w_out_ref[...], 0.0)
    pre_grad = (w_out * gate * (1.0 + pre * (1.0 - gate))).astype(BF16)
    back_all = dot_nt(pre_grad, w_all)
    back_left, back_right = back_all[:, :SLOTS], back_all[:, SLOTS:]
    part_left = jnp.where(low, back_left, 2.0 * left * back_left)
    part_right = 2.0 * right * back_right
    fold = own_left * part_left + own_right * part_right
    fold = fold + pltpu.roll(fold, CHANNELS, 1)
    full = jnp.concatenate([part_left - jnp.where(low, fold, 0.0), part_right], axis=1)
    half = (0.5 * KAPPA) * scalar
    fi[0] = jnp.where(low, 0.0, half * part_left)
    fi[1] = jnp.where(low, half * part_right, 0.0)
    fi[2] = jnp.where(low, 0.0, half * part_right)
    for block in range(CHUNKS):
        piece = full[block * CHUNK : (block + 1) * CHUNK]
        for k in range(NBASIS):
            base = block * 4 * CHUNK + k * CHUNK
            scaled = weights_k[k] * piece
            grad[base : base + CHUNK] = scaled.astype(BF16)
    gradt[...] = dot_nt(swap_ref[...], grad[...]).astype(BF16)
    pre_ref[...] = pre_grad
    heat_ref[...] = pre * gate * w_out
    backward_tiles(trips, tables, xi, xj, saved, grad, gradt, pbuf, bbuf, fi, cg, pg)
    slots = [0, 1]
    if sizes[0] > 2 and sizes[0] % 2 == 0:
        odd = lax.rem(lax.axis_index("gx"), 2)
        slots = [1 - odd, odd]
    write_out(out_refs, counts, cg, pg, slots)


def rest_kernel(sizes, counts, *refs):
    nyu = counts[1]
    list_ref, xi, xj, *saved = refs[:8]
    grad, gradt, fi_in = refs[8:11]
    out_refs = refs[11 : 11 + nyu]
    cell_of, slot_of, shift_of, pbuf, bbuf, fi, cg, pg = refs[11 + nyu :]
    tables = (cell_of, slot_of, shift_of)
    trips = tabulate(lambda tile: list_ref[0, 0, 0, tile], tables, False, sizes, counts)
    fi[...] = fi_in[...]
    backward_tiles(trips, tables, xi, xj, saved, grad, gradt, pbuf, bbuf, fi, cg, pg)
    for axis in range(3):
        pg[0, axis : axis + 1] -= (2.0 / KAPPA) * row_sums(fi[axis])
    write_out(out_refs, counts, cg, pg, [0])


def direct_kernel(sizes, counts, pre_ref, heat_ref, w_hidden_ref, energy_ref, direct_ref):
    energy_ref[0, 0] = row_sums(heat_ref[...])
    direct_ref[...] = dot_nt(pre_ref[...], w_hidden_ref[...])


def finish_kernel(count, *refs):
    keep_ref = refs[0]
    got_refs = refs[1 : 1 + count]
    direct_ref, w_env_ref, force_ref, grad_ref = refs[1 + count :]
    total = keep_ref[0]
    for got in got_refs:
        total = total + got[0].astype(F32)
    chan = total[:CHANNELS]
    high = chan.astype(BF16)
    low = (chan - high.astype(F32)).astype(BF16)
    both = jnp.concatenate([high, low], axis=0)
    w_env = w_env_ref[...]
    weights = jnp.concatenate([w_env, w_env], axis=0)
    part = lax.dot_general(both, weights, (((0,), (0,)), ((), ())), preferred_element_type=F32)
    grad_ref[0, 0, 0] = (direct_ref[...] + part).astype(BF16)
    for axis in range(3):
        force_ref[0, 0, axis] = -total[POS_ROW + axis : POS_ROW + axis + 1]


def shifted(value, axis, steps):
    count = lax.axis_size(axis)
    return lax.ppermute(value, axis, [(i, (i + steps) % count) for i in range(count)])


def gathered(value, axis):
    if lax.axis_size(axis) == 2:
        return [value, shifted(value, axis, 1)]
    up = shifted(value, axis, -1)
    down = shifted(value, axis, 1)
    return [value, up, down]


def returned(parts, axis):
    count = lax.axis_size(axis)
    if count == 2:
        return [shifted(parts[0], axis, 1)]
    return [shifted(parts[1], axis, -1), shifted(parts[0], axis, 1)]


def swapped(parts, axis):
    count = lax.axis_size(axis)
    if count == 2 or count % 2:
        return returned(parts, axis)
    ring = [(i, ((((i + 1) % count) ^ 1) - 1) % count) for i in range(count)]
    far = lax.ppermute(parts[0], axis, ring)
    near = lax.ppermute(parts[1], axis, [(i, i ^ 1) for i in range(count)])
    return [far, near]


VMEM = pl.BlockSpec(memory_space=pltpu.VMEM)
SMEM = pl.BlockSpec(memory_space=pltpu.SMEM)
SMALL = pltpu.CompilerParams(vmem_limit_bytes=4 << 20)


def layer(
    feats, positions, species, cell_counts, pair_list, w_env, radial, pair_scale, w_hidden,
    w_zero, w_one, w_out,
):
    sizes = [lax.axis_size(axis) for axis in ("gx", "gy", "gz")]
    nxu, nyu, nzu = [2 if size == 2 else 3 for size in sizes]
    msg = pl.pallas_call(
        pack_kernel,
        out_shape=jax.ShapeDtypeStruct((1, ROWS, SLOTS), BF16),
        in_specs=[VMEM] * 7,
        out_specs=VMEM,
        scratch_shapes=[pltpu.VMEM((8, SLOTS), F32)],
        name="pack",
    )(
        cell_counts, feats, positions.transpose(0, 1, 3, 2, 4), species, w_env.T, pair_list,
        pair_scale,
    )
    stack = gathered(msg, "gz")
    column = jnp.pad(msg, ((0, 0), (0, ROWS * (nzu - 1)), (0, 0)))
    column = lax.optimization_barrier(column)
    for uz in range(1, nzu):
        column = lax.dynamic_update_slice(column, stack[uz], (0, uz * ROWS, 0))
    blocks = [gathered(part, "gy") for part in gathered(column, "gx")]
    near_blocks = blocks[0]
    far_blocks = [block for part in blocks[1:] for block in part]
    counts = (nxu, nyu, nzu)
    near_cells, far_cells = nyu * nzu, (nxu - 1) * nyu * nzu

    def table_scratch():
        return [
            pltpu.SMEM((OFFSETS + 5,), jnp.int32),
            pltpu.SMEM((OFFSETS + 5,), jnp.int32),
            pltpu.SMEM((3, OFFSETS + 5), F32),
        ]

    def saved_shapes(pairs):
        return [
            ((pairs, QUAD, LANES), BF16),
            ((pairs + 1, WIDE, LANES), BF16),
            ((pairs, SLOTS, LANES), F32),
            ((pairs, SLOTS, LANES), F32),
            ((pairs, SLOTS, LANES), F32),
        ]

    square = (SLOTS, SLOTS)
    now_scratch = [pltpu.VMEM((QUAD, LANES), BF16), pltpu.VMEM((WIDE, LANES), BF16)]
    buffers = [pltpu.VMEM((QUAD, WIDE), F32), pltpu.VMEM((WIDE, LANES), F32)]

    def sums_scratch(cells):
        return [pltpu.VMEM((cells, CHANNELS, SLOTS), F32), pltpu.VMEM((cells, 8, SLOTS), F32)]

    def call(kernel, shapes, scratch, megabytes, first, *operands):
        return pl.pallas_call(
            lambda *refs: kernel(sizes, counts, *refs),
            out_shape=[jax.ShapeDtypeStruct(*shape) for shape in shapes],
            in_specs=first + [VMEM] * (len(operands) - len(first)),
            out_specs=[VMEM] * len(shapes),
            scratch_shapes=scratch,
            compiler_params=pltpu.CompilerParams(vmem_limit_bytes=megabytes << 20),
            cost_estimate=pl.CostEstimate(
                flops=1000000000, bytes_accessed=4000000, transcendentals=0
            ),
        )(*operands)

    inner = call(
        inner_kernel,
        [
            ((3,) + square, F32),
            (square, F32),
            (square, BF16),
            ((near_cells, 8, SLOTS), F32),
            ((QUAD, WIDE), F32),
        ]
        + saved_shapes(NEAR_PAIRS),
        table_scratch()
        + [pltpu.VMEM((near_cells + 1,) + square, F32)]
        + [pltpu.VMEM((near_cells, CHANNELS, SLOTS), BF16)]
        + now_scratch
        + [
            pltpu.VMEM((1, SLOTS), jnp.int32),
            pltpu.SMEM((1, SLOTS), jnp.int32),
            pltpu.SemaphoreType.DMA,
        ],
        12,
        [],
        *near_blocks,
    )
    xi, code, onehot, xj, acc = inner[:5]
    saved = inner[5:]
    place = jnp.arange(WIDE)
    held = place % CHUNK + place // (4 * CHUNK) * CHUNK + place // CHUNK % 4 * CHANNELS
    swap = (held[:, None] == place[None, :]).astype(BF16)
    far_out = (nxu - 1) * nzu
    outer = call(
        outer_kernel,
        [
            ((QUAD, WIDE), BF16),
            ((WIDE, QUAD), BF16),
            ((3,) + square, F32),
            ((SLOTS, D), BF16),
            ((SLOTS, D), F32),
            ((far_out, ROWS, SLOTS), F32),
        ]
        + [((far_out, ROWS, SLOTS), BF16)] * (nyu - 1),
        table_scratch()
        + [pltpu.VMEM((far_cells + 1,) + square, F32)]
        + [pltpu.VMEM((far_cells, 8, SLOTS), F32)]
        + [pltpu.VMEM((far_cells, CHANNELS, SLOTS), BF16)]
        + [pltpu.VMEM(*shape) for shape in saved_shapes(FAR_PAIRS)]
        + [pltpu.VMEM((QUAD, WIDE), F32)]
        + buffers
        + now_scratch
        + sums_scratch(far_cells)
        + [pltpu.VMEM((SLOTS, D), F32)],
        20,
        [SMEM],
        pair_list, *far_blocks, pair_scale, radial, w_zero, w_one, w_out.reshape(1, D), swap,
        feats, w_hidden, xi, code, onehot, acc,
    )
    grad, gradt, force_in, pre_grad, heat = outer[:5]
    total = outer[5]
    for got in returned(outer[6:], "gy"):
        total = total + got.astype(F32)
    sends = [total[ux * nzu : (ux + 1) * nzu].astype(BF16) for ux in range(nxu - 1)]
    from_far = swapped(sends, "gx")
    rest = call(
        rest_kernel,
        [((nzu, ROWS, SLOTS), F32)] + [((nzu, ROWS, SLOTS), BF16)] * (nyu - 1),
        table_scratch()
        + buffers
        + [pltpu.VMEM((3,) + square, F32)]
        + sums_scratch(near_cells),
        12,
        [SMEM],
        pair_list, xi, xj, *saved, grad, gradt, force_in,
    )
    energy, direct = call(
        direct_kernel,
        [((1, 1, 1, SLOTS), F32), ((SLOTS, D), F32)],
        [],
        4,
        [],
        pre_grad, heat, w_hidden,
    )
    total = rest[0]
    for got in returned(rest[1:], "gy"):
        total = total + got.astype(F32)
    for got in from_far:
        total = total + got.astype(F32)
    sends = [total[uz : uz + 1].astype(BF16) for uz in range(1, nzu)]
    keep = total[:1]
    arrived = returned(sends, "gz")
    forces, feat_grad = pl.pallas_call(
        lambda *refs: finish_kernel(len(arrived), *refs),
        out_shape=[
            jax.ShapeDtypeStruct((1, 1, 3, 1, SLOTS), F32),
            jax.ShapeDtypeStruct((1, 1, 1, SLOTS, D), BF16),
        ],
        in_specs=[VMEM] * (3 + len(arrived)),
        out_specs=[VMEM] * 2,
        compiler_params=SMALL,
        name="finish",
    )(keep, *arrived, direct, w_env.T)
    return energy, forces.transpose(0, 1, 3, 2, 4), feat_grad


def solution(mesh):
    cell = P("gx", "gy", "gz")
    in_specs = (cell,) * 5 + (P(),) * 7
    return jax.shard_map(
        layer, mesh=mesh, in_specs=in_specs, out_specs=(cell,) * 3, check_vma=False
    )
```

```python
import jax
import jax.numpy as jnp
from jax import lax
from jax.experimental import pallas as pl
from jax.experimental.pallas import tpu as pltpu
from jax.sharding import PartitionSpec as P


D = 256
CHANNELS = 64
NBASIS = 4
NSPEC = 6
SLOTS = 128
CUTOFF = 0.55
CENTRE = 0.5
ROWS = 80
POS_ROW = 64
EXTRA_ROW = 74
LIST_LANE = 32
OFFSETS = 27
CHUNK = 16
CHUNKS = SLOTS // CHUNK
QUAD = NBASIS * SLOTS
WIDE = 4 * CHANNELS
LANES = 2 * SLOTS
NEAR_PAIRS = 5
FAR_PAIRS = 9
TOP = 8.0 * 1.4426950408889634
KAPPA = TOP**0.5
SLOPE = 4.0 * 1.4426950408889634**0.5 / TOP
SHIFT = 0.5 * 1.4426950408889634**0.5
LADDER = (1.0, 0.1353352832366127, 0.0024787521766663585, 6.14421235332821e-06)
F32 = jnp.float32
BF16 = jnp.bfloat16


def dot_nn(a, b):
    return lax.dot_general(a, b, (((1,), (0,)), ((), ())), preferred_element_type=F32)


def dot_nt(a, b):
    return lax.dot_general(a, b, (((1,), (1,)), ((), ())), preferred_element_type=F32)


def split3(value):
    high = value.astype(BF16)
    rest = value - high.astype(F32)
    middle = rest.astype(BF16)
    low = (rest - middle.astype(F32)).astype(BF16)
    return high, middle, low


def pack_kernel(
    counts_ref, feats_ref, pos_ref, species_ref, w_env_ref, list_ref, scale_ref, msg_ref, extra
):
    chans = dot_nt(w_env_ref[...], feats_ref[0, 0, 0])
    msg_ref[0, :CHANNELS] = chans.astype(BF16)
    pos = jnp.concatenate([pos_ref[0, 0, axis] for axis in range(3)], axis=0)
    slots = lax.broadcasted_iota(jnp.int32, (1, SLOTS), 1)
    counts = jnp.broadcast_to(counts_ref[0], (1, SLOTS))
    code = jnp.where(slots < counts, species_ref[0, 0].astype(F32), -1.0)
    high = pos.astype(BF16).astype(F32)
    middle = (pos - high).astype(BF16).astype(F32)
    low = pos - high - middle
    extra[...] = jnp.zeros_like(extra)
    for piece, value in enumerate(split3(scale_ref[...])):
        extra[:NSPEC, 8 * piece : 8 * piece + NSPEC] = value.astype(F32)
    extra[:1, LIST_LANE : LIST_LANE + OFFSETS] = list_ref[0, 0].astype(F32)
    tail = jnp.concatenate([high, middle, low, code, extra[:NSPEC]], axis=0)
    msg_ref[0, CHANNELS:] = tail.astype(BF16)


def row_sums(value):
    ones = jnp.ones((8, value.shape[1]), BF16)
    high, middle, low = split3(value)
    total = dot_nt(ones, high) + dot_nt(ones, middle) + dot_nt(ones, low)
    return total[0:1]


def unique_of(offset, count):
    if offset == 0 or count == 2:
        return abs(offset)
    return 1 if offset > 0 else 2


def tabulate(listed, tables, zone, sizes, counts):
    cell_of, slot_of, shift_of = tables
    nxu, nyu, nzu = counts
    live = jnp.int32(0)
    for tile in range(OFFSETS):
        offset = (tile // 9 - 1, tile // 3 % 3 - 1, tile % 3 - 1)
        if (offset[0] != 0) != zone:
            continue
        ux, uy, uz = [unique_of(o, size) for o, size in zip(offset, sizes)]
        cell = (max(ux - 1, 0) * nzu + uz) * nyu + uy
        cell_of[live] = jnp.int32(cell)
        slot_of[live] = jnp.int32(cell)
        for axis in range(3):
            shift_of[axis, live] = jnp.float32(offset[axis] * KAPPA / CUTOFF)
        live = live + listed(tile)
    for spare in (live, live + 1):
        cell_of[spare] = jnp.int32(0)
        slot_of[spare] = jnp.int32((nxu - 1 if zone else 1) * nyu * nzu)
        for axis in range(3):
            shift_of[axis, spare] = jnp.float32(0.0)
    return (live + 1) // 2


def unpack(msg_refs, counts, xj, chan):
    nyu, nzu = counts[1:]
    codes = []
    for cell in range(xj.shape[0]):
        msg = msg_refs[cell // (nyu * nzu) * nyu + cell % nyu]
        at = cell // nyu % nzu * ROWS
        tail = msg[0, at + CHANNELS : at + ROWS].astype(F32)
        place = tail[0:3] + tail[3:6] + tail[6:9]
        xj[cell, 0:3] = (place - CENTRE) * (KAPPA / CUTOFF)
        codes.append(tail[9:10])
        chan[cell] = msg[0, at : at + CHANNELS]
    return codes


def strengths(codes, onehot, scale, weight):
    scale = scale * (1.0 / (TOP * TOP))
    scale = jnp.concatenate([scale, jnp.zeros((8 - NSPEC, NSPEC), F32)], axis=0)
    coef = []
    for code in codes:
        total = jnp.zeros((8, SLOTS), F32)
        for kind in range(NSPEC):
            column = jnp.broadcast_to(scale[:, kind : kind + 1], (8, SLOTS))
            total = total + jnp.where(code == float(kind), column, 0.0)
        high = total.astype(BF16).astype(F32)
        middle = (total - high).astype(BF16).astype(F32)
        low = total - high - middle
        coef.append(
            jnp.concatenate([high, middle, low, jnp.zeros((104, SLOTS), F32)], axis=0).astype(BF16)
        )
    for cell in range(0, len(codes), 2):
        strength = dot_nn(onehot, jnp.concatenate(coef[cell : cell + 2], axis=1))
        weight[cell] = strength[:, :SLOTS]
        if cell + 1 < len(codes):
            weight[cell + 1] = strength[:, SLOTS:]
    weight[len(codes)] = jnp.zeros((SLOTS, SLOTS), F32)


def rows_of(pair, tables, xj):
    cell_of, slot_of, shift_of = tables
    first, second = 2 * pair, 2 * pair + 1
    cell_a, cell_b = cell_of[first], cell_of[second]
    rows = [
        jnp.concatenate(
            [
                xj[cell_a, axis : axis + 1] + shift_of[axis, first],
                xj[cell_b, axis : axis + 1] + shift_of[axis, second],
            ],
            axis=1,
        )
        for axis in range(3)
    ]
    return cell_a, cell_b, slot_of[first], slot_of[second], rows


def relative(rows, xi, block):
    out = []
    for axis in range(3):
        own = xi[axis, block * CHUNK : (block + 1) * CHUNK]
        out.append(rows[axis] - jnp.concatenate([own, own], axis=1))
    return out


def forward_tiles(trips, tables, xi, xj, chan, weight, saved, acc):
    tiles, rmat, s_all, r_all, wb_all = saved

    def forward(pair, carry):
        cell_a, cell_b, weight_a, weight_b, rows = rows_of(pair, tables, xj)
        values = jnp.concatenate([chan[cell_a], chan[cell_b]], axis=1)
        rmat[pair, :CHANNELS] = values
        wide = values.astype(F32)
        for axis in range(3):
            base = (axis + 1) * CHANNELS
            scaled = (wide * rows[axis]).astype(BF16)
            rmat[pair, base : base + CHANNELS] = scaled
        for block in range(CHUNKS):
            at = slice(block * CHUNK, (block + 1) * CHUNK)
            dx, dy, dz = relative(rows, xi, block)
            s = jnp.minimum(dx * dx + dy * dy + dz * dz, TOP)
            inside = TOP - s
            spread = SLOPE * s - SHIFT
            ratio = jnp.exp2(s)
            strength = jnp.concatenate([weight[weight_a, at], weight[weight_b, at]], axis=1)
            wb = strength * jnp.exp2(-(spread * spread))
            s_all[pair, at] = s
            r_all[pair, at] = ratio
            wb_all[pair, at] = wb
            tile = wb * (inside * inside)
            for k in range(NBASIS):
                base = block * 4 * CHUNK + k * CHUNK
                rounded = tile.astype(BF16)
                tiles[pair, base : base + CHUNK] = rounded
                if k + 1 < NBASIS:
                    tile = tile * ratio
        acc[...] += dot_nt(tiles[pair], rmat[pair])
        return carry

    lax.fori_loop(0, trips, forward, 0)


def backward_tiles(trips, tables, xi, xj, saved, grad, gradt, pbuf, bbuf, fi, cg, pg):
    tiles, rmat, s_all, r_all, wb_all = saved
    pbuf[...] = dot_nn(grad[...], rmat[0])
    bbuf[...] = jnp.zeros_like(bbuf)
    cg[...] = jnp.zeros_like(cg)
    pg[...] = jnp.zeros_like(pg)

    def settle(pair):
        cell_a, cell_b, _, _, rows = rows_of(pair, tables, xj)
        along = [jnp.zeros((CHUNK, LANES), F32) for _ in range(3)]
        for part in range(CHANNELS // CHUNK):
            at = slice(part * CHUNK, (part + 1) * CHUNK)
            values = rmat[pair, at].astype(F32)
            sums = bbuf[part * 4 * CHUNK : part * 4 * CHUNK + CHUNK]
            for axis in range(3):
                base = part * 4 * CHUNK + (axis + 1) * CHUNK
                piece = bbuf[base : base + CHUNK]
                sums = sums + rows[axis] * piece
                along[axis] = along[axis] + values * piece
            cg[cell_a, at] += sums[:, :SLOTS]
            cg[cell_b, at] += sums[:, SLOTS:]
        for axis in range(3):
            total = KAPPA * jnp.sum(along[axis], axis=0, keepdims=True)
            pg[cell_a, axis : axis + 1] += total[:, :SLOTS]
            pg[cell_b, axis : axis + 1] += total[:, SLOTS:]

    def backward(pair, carry):
        cell_a, cell_b, _, _, rows = rows_of(pair, tables, xj)
        settle(jnp.maximum(pair - 1, 0))
        bbuf[...] = dot_nn(gradt[...], tiles[pair])
        totals = [jnp.zeros((CHUNK, LANES), F32) for _ in range(3)]
        for block in range(CHUNKS):
            at = slice(block * CHUNK, (block + 1) * CHUNK)
            s = s_all[pair, at]
            ratio = r_all[pair, at]
            inside = TOP - s
            step = 8.0 * inside
            level = -2.0 * TOP - inside * ((32.0 / TOP) * s - 4.0)
            levels = [level]
            for _ in range(1, NBASIS):
                levels.append(levels[-1] + step)
            base = block * 4 * CHUNK
            slope = levels[3] * pbuf[base + 3 * CHUNK : base + 4 * CHUNK]
            for k in (2, 1, 0):
                slope = slope * ratio + levels[k] * pbuf[base + k * CHUNK : base + (k + 1) * CHUNK]
            slope = slope * (wb_all[pair, at] * inside)
            for axis, delta in enumerate(relative(rows, xi, block)):
                push = slope * delta
                totals[axis] = totals[axis] + push
                fi[axis, at] += push[:, :SLOTS] + push[:, SLOTS:]
        for axis in range(3):
            total = (2.0 / KAPPA) * jnp.sum(totals[axis], axis=0, keepdims=True)
            pg[cell_a, axis : axis + 1] += total[:, :SLOTS]
            pg[cell_b, axis : axis + 1] += total[:, SLOTS:]
        pbuf[...] = dot_nn(grad[...], rmat[pair + 1])
        return carry

    lax.fori_loop(0, trips, backward, 0)

    @pl.when(trips > 0)
    def _():
        settle(trips - 1)


def write_out(out_refs, counts, cg, pg, slots):
    nyu, nzu = counts[1:]
    for cell in range(cg.shape[0]):
        out = out_refs[cell % nyu]
        at = slots[cell // (nyu * nzu)] * nzu + cell // nyu % nzu
        out[at, :CHANNELS] = cg[cell].astype(out.dtype)
        tail = jnp.concatenate([pg[cell], jnp.zeros((8, SLOTS), F32)], axis=0)
        out[at, CHANNELS:] = (tail * (1.0 / CUTOFF)).astype(out.dtype)


def inner_kernel(sizes, counts, *refs):
    _, nyu, _ = counts
    msg_refs = refs[:nyu]
    xi, code_ref, onehot_ref, xj, acc, *saved = refs[nyu : 10 + nyu]
    (cell_of, slot_of, shift_of, weight, chan, _, _, list_row, list_ref, sem) = refs[10 + nyu :]
    tables = (cell_of, slot_of, shift_of)
    tail = msg_refs[0][0, CHANNELS:ROWS].astype(F32)
    extra = tail[EXTRA_ROW - CHANNELS : EXTRA_ROW - CHANNELS + NSPEC]
    list_row[...] = extra[:1].astype(jnp.int32)
    list_copy = pltpu.make_async_copy(list_row, list_ref, sem)
    list_copy.start()
    scale = extra[:, :NSPEC] + extra[:, 8 : 8 + NSPEC] + extra[:, 16 : 16 + NSPEC]
    codes = unpack(msg_refs, counts, xj, chan)
    for axis in range(3):
        xi[axis] = jnp.broadcast_to(xj[0, axis : axis + 1], (SLOTS, SLOTS)).T
    code_i = jnp.broadcast_to(codes[0], (SLOTS, SLOTS)).T
    code_ref[...] = code_i
    lane = lax.broadcasted_iota(jnp.int32, (SLOTS, SLOTS), 1)
    sub = lax.broadcasted_iota(jnp.int32, (SLOTS, SLOTS), 0)
    onehot = jnp.where((code_i == (lane % 8).astype(F32)) & (lane < 24), 1.0, 0.0)
    onehot = onehot.astype(BF16)
    onehot_ref[...] = onehot
    strengths(codes, onehot, scale, weight)
    list_copy.wait()
    trips = tabulate(lambda tile: list_ref[0, LIST_LANE + tile], tables, False, sizes, counts)
    weight[0] = jnp.where(lane == sub, 0.0, weight[0])
    acc[...] = jnp.zeros_like(acc)
    forward_tiles(trips, tables, xi, xj, chan, weight, saved, acc)


def outer_kernel(sizes, counts, *refs):
    nxu, nyu, _ = counts
    far = (nxu - 1) * nyu
    list_ref, msg_refs = refs[0], refs[1 : 1 + far]
    refs = refs[1 + far :]
    scale_ref, radial_ref, w_zero_ref, w_one_ref, w_out_ref, swap_ref = refs[:6]
    feats_ref, w_hidden_ref, xi, code_ref, onehot_ref, acc_in = refs[6:12]
    grad, gradt, fi, pre_ref, heat_ref = refs[12:17]
    out_refs = refs[17 : 17 + nyu]
    (
        cell_of, slot_of, shift_of, weight, xj, chan, tiles, rmat, s_all, r_all, wb_all,
        acc, pbuf, bbuf, _, _, cg, pg, hbuf,
    ) = refs[17 + nyu :]
    tables = (cell_of, slot_of, shift_of)
    saved = (tiles, rmat, s_all, r_all, wb_all)
    trips = tabulate(lambda tile: list_ref[0, 0, 0, tile], tables, True, sizes, counts)
    codes = unpack(msg_refs, counts, xj, chan)
    strengths(codes, onehot_ref[...], scale_ref[...], weight)
    acc[...] = acc_in[...]
    hbuf[...] = dot_nn(feats_ref[0, 0, 0], w_hidden_ref[...])
    forward_tiles(trips, tables, xi, xj, chan, weight, saved, acc)

    radial = radial_ref[...]
    weights_k = []
    for k in range(NBASIS):
        row = radial[k : k + 1] * LADDER[k]
        weights_k.append(jnp.concatenate([row] + [row * (1.0 / KAPPA)] * 3, axis=1))
    mixed = []
    for block in range(CHUNKS):
        base = block * 4 * CHUNK
        total = weights_k[0] * acc[base : base + CHUNK]
        for k in range(1, NBASIS):
            total = total + weights_k[k] * acc[base + k * CHUNK : base + (k + 1) * CHUNK]
        mixed.append(total)
    mixed = jnp.concatenate(mixed, axis=0)
    low = lax.broadcasted_iota(jnp.int32, (SLOTS, SLOTS), 1) < CHANNELS
    left, right = mixed[:, :SLOTS], mixed[:, SLOTS:]
    scalar = jnp.where(low, left, pltpu.roll(left, CHANNELS, 1))
    own_left = jnp.where(low, 0.0, xi[0]) * (1.0 / KAPPA)
    own_right = jnp.where(low, xi[1], xi[2]) * (1.0 / KAPPA)
    left = left - own_left * scalar
    right = right - own_right * scalar
    features = [jnp.where(low, left, left * left), right * right]
    features = jnp.concatenate(features, axis=1).astype(BF16)
    w_one = w_one_ref[...]
    w_all = jnp.concatenate([w_zero_ref[...], w_one, w_one, w_one], axis=0)
    pre = hbuf[...] + dot_nn(features, w_all)
    gate = jax.nn.sigmoid(pre)
    occupied = jnp.concatenate([code_ref[...], code_ref[...]], axis=1) >= 0.0
    w_out = jnp.where(occupied, w_out_ref[...], 0.0)
    pre_grad = (w_out * gate * (1.0 + pre * (1.0 - gate))).astype(BF16)
    back_all = dot_nt(pre_grad, w_all)
    back_left, back_right = back_all[:, :SLOTS], back_all[:, SLOTS:]
    part_left = jnp.where(low, back_left, 2.0 * left * back_left)
    part_right = 2.0 * right * back_right
    fold = own_left * part_left + own_right * part_right
    fold = fold + pltpu.roll(fold, CHANNELS, 1)
    full = jnp.concatenate([part_left - jnp.where(low, fold, 0.0), part_right], axis=1)
    half = (0.5 * KAPPA) * scalar
    fi[0] = jnp.where(low, 0.0, half * part_left)
    fi[1] = jnp.where(low, half * part_right, 0.0)
    fi[2] = jnp.where(low, 0.0, half * part_right)
    for block in range(CHUNKS):
        piece = full[block * CHUNK : (block + 1) * CHUNK]
        for k in range(NBASIS):
            base = block * 4 * CHUNK + k * CHUNK
            scaled = weights_k[k] * piece
            grad[base : base + CHUNK] = scaled.astype(BF16)
    gradt[...] = dot_nt(swap_ref[...], grad[...]).astype(BF16)
    pre_ref[...] = pre_grad
    heat_ref[...] = pre * gate * w_out
    backward_tiles(trips, tables, xi, xj, saved, grad, gradt, pbuf, bbuf, fi, cg, pg)
    slots = [0, 1]
    if sizes[0] > 2 and sizes[0] % 2 == 0:
        odd = lax.rem(lax.axis_index("gx"), 2)
        slots = [1 - odd, odd]
    write_out(out_refs, counts, cg, pg, slots)


def rest_kernel(sizes, counts, *refs):
    nyu = counts[1]
    list_ref, xi, xj, *saved = refs[:8]
    grad, gradt, fi_in = refs[8:11]
    out_refs = refs[11 : 11 + nyu]
    cell_of, slot_of, shift_of, pbuf, bbuf, fi, cg, pg = refs[11 + nyu :]
    tables = (cell_of, slot_of, shift_of)
    trips = tabulate(lambda tile: list_ref[0, 0, 0, tile], tables, False, sizes, counts)
    fi[...] = fi_in[...]
    backward_tiles(trips, tables, xi, xj, saved, grad, gradt, pbuf, bbuf, fi, cg, pg)
    for axis in range(3):
        pg[0, axis : axis + 1] -= (2.0 / KAPPA) * row_sums(fi[axis])
    write_out(out_refs, counts, cg, pg, [0])


def direct_kernel(sizes, counts, pre_ref, heat_ref, w_hidden_ref, energy_ref, direct_ref):
    energy_ref[0, 0] = row_sums(heat_ref[...])
    direct_ref[...] = dot_nt(pre_ref[...], w_hidden_ref[...])


def finish_kernel(count, *refs):
    keep_ref = refs[0]
    got_refs = refs[1 : 1 + count]
    direct_ref, w_env_ref, force_ref, grad_ref = refs[1 + count :]
    total = keep_ref[0]
    for got in got_refs:
        total = total + got[0].astype(F32)
    chan = total[:CHANNELS]
    high = chan.astype(BF16)
    low = (chan - high.astype(F32)).astype(BF16)
    both = jnp.concatenate([high, low], axis=0)
    w_env = w_env_ref[...]
    weights = jnp.concatenate([w_env, w_env], axis=0)
    part = lax.dot_general(both, weights, (((0,), (0,)), ((), ())), preferred_element_type=F32)
    grad_ref[0, 0, 0] = (direct_ref[...] + part).astype(BF16)
    for axis in range(3):
        force_ref[0, 0, axis] = -total[POS_ROW + axis : POS_ROW + axis + 1]


def shifted(value, axis, steps):
    count = lax.axis_size(axis)
    return lax.ppermute(value, axis, [(i, (i + steps) % count) for i in range(count)])


def gathered(value, axis):
    if lax.axis_size(axis) == 2:
        return [value, shifted(value, axis, 1)]
    up = shifted(value, axis, -1)
    down = shifted(value, axis, 1)
    return [value, up, down]


def returned(parts, axis):
    count = lax.axis_size(axis)
    if count == 2:
        return [shifted(parts[0], axis, 1)]
    return [shifted(parts[1], axis, -1), shifted(parts[0], axis, 1)]


def swapped(parts, axis):
    count = lax.axis_size(axis)
    if count == 2 or count % 2:
        return returned(parts, axis)
    ring = [(i, ((((i + 1) % count) ^ 1) - 1) % count) for i in range(count)]
    far = lax.ppermute(parts[0], axis, ring)
    near = lax.ppermute(parts[1], axis, [(i, i ^ 1) for i in range(count)])
    return [far, near]


VMEM = pl.BlockSpec(memory_space=pltpu.VMEM)
SMEM = pl.BlockSpec(memory_space=pltpu.SMEM)
SMALL = pltpu.CompilerParams(vmem_limit_bytes=4 << 20)


def layer(
    feats, positions, species, cell_counts, pair_list, w_env, radial, pair_scale, w_hidden,
    w_zero, w_one, w_out,
):
    sizes = [lax.axis_size(axis) for axis in ("gx", "gy", "gz")]
    nxu, nyu, nzu = [2 if size == 2 else 3 for size in sizes]
    msg = pl.pallas_call(
        pack_kernel,
        out_shape=jax.ShapeDtypeStruct((1, ROWS, SLOTS), BF16),
        in_specs=[VMEM] * 7,
        out_specs=VMEM,
        scratch_shapes=[pltpu.VMEM((8, SLOTS), F32)],
        name="pack",
    )(
        cell_counts, feats, positions.transpose(0, 1, 3, 2, 4), species, w_env.T, pair_list,
        pair_scale,
    )
    stack = gathered(msg, "gz")
    column = jnp.pad(msg, ((0, 0), (0, ROWS * (nzu - 1)), (0, 0)))
    column = lax.optimization_barrier(column)
    for uz in range(1, nzu):
        column = lax.dynamic_update_slice(column, stack[uz], (0, uz * ROWS, 0))
    blocks = [gathered(part, "gy") for part in gathered(column, "gx")]
    near_blocks = blocks[0]
    far_blocks = [block for part in blocks[1:] for block in part]
    counts = (nxu, nyu, nzu)
    near_cells, far_cells = nyu * nzu, (nxu - 1) * nyu * nzu

    def table_scratch():
        return [
            pltpu.SMEM((OFFSETS + 5,), jnp.int32),
            pltpu.SMEM((OFFSETS + 5,), jnp.int32),
            pltpu.SMEM((3, OFFSETS + 5), F32),
        ]

    def saved_shapes(pairs):
        return [
            ((pairs, QUAD, LANES), BF16),
            ((pairs + 1, WIDE, LANES), BF16),
            ((pairs, SLOTS, LANES), F32),
            ((pairs, SLOTS, LANES), F32),
            ((pairs, SLOTS, LANES), F32),
        ]

    square = (SLOTS, SLOTS)
    now_scratch = [pltpu.VMEM((QUAD, LANES), BF16), pltpu.VMEM((WIDE, LANES), BF16)]
    buffers = [pltpu.VMEM((QUAD, WIDE), F32), pltpu.VMEM((WIDE, LANES), F32)]

    def sums_scratch(cells):
        return [pltpu.VMEM((cells, CHANNELS, SLOTS), F32), pltpu.VMEM((cells, 8, SLOTS), F32)]

    def call(kernel, shapes, scratch, megabytes, first, *operands):
        return pl.pallas_call(
            lambda *refs: kernel(sizes, counts, *refs),
            out_shape=[jax.ShapeDtypeStruct(*shape) for shape in shapes],
            in_specs=first + [VMEM] * (len(operands) - len(first)),
            out_specs=[VMEM] * len(shapes),
            scratch_shapes=scratch,
            compiler_params=pltpu.CompilerParams(vmem_limit_bytes=megabytes << 20),
            cost_estimate=pl.CostEstimate(
                flops=1000000000, bytes_accessed=4000000, transcendentals=0
            ),
        )(*operands)

    inner = call(
        inner_kernel,
        [
            ((3,) + square, F32),
            (square, F32),
            (square, BF16),
            ((near_cells, 8, SLOTS), F32),
            ((QUAD, WIDE), F32),
        ]
        + saved_shapes(NEAR_PAIRS),
        table_scratch()
        + [pltpu.VMEM((near_cells + 1,) + square, F32)]
        + [pltpu.VMEM((near_cells, CHANNELS, SLOTS), BF16)]
        + now_scratch
        + [
            pltpu.VMEM((1, SLOTS), jnp.int32),
            pltpu.SMEM((1, SLOTS), jnp.int32),
            pltpu.SemaphoreType.DMA,
        ],
        12,
        [],
        *near_blocks,
    )
    xi, code, onehot, xj, acc = inner[:5]
    saved = inner[5:]
    place = jnp.arange(WIDE)
    held = place % CHUNK + place // (4 * CHUNK) * CHUNK + place // CHUNK % 4 * CHANNELS
    swap = (held[:, None] == place[None, :]).astype(BF16)
    far_out = (nxu - 1) * nzu
    outer = call(
        outer_kernel,
        [
            ((QUAD, WIDE), BF16),
            ((WIDE, QUAD), BF16),
            ((3,) + square, F32),
            ((SLOTS, D), BF16),
            ((SLOTS, D), F32),
            ((far_out, ROWS, SLOTS), F32),
        ]
        + [((far_out, ROWS, SLOTS), BF16)] * (nyu - 1),
        table_scratch()
        + [pltpu.VMEM((far_cells + 1,) + square, F32)]
        + [pltpu.VMEM((far_cells, 8, SLOTS), F32)]
        + [pltpu.VMEM((far_cells, CHANNELS, SLOTS), BF16)]
        + [pltpu.VMEM(*shape) for shape in saved_shapes(FAR_PAIRS)]
        + [pltpu.VMEM((QUAD, WIDE), F32)]
        + buffers
        + now_scratch
        + sums_scratch(far_cells)
        + [pltpu.VMEM((SLOTS, D), F32)],
        20,
        [SMEM],
        pair_list, *far_blocks, pair_scale, radial, w_zero, w_one, w_out.reshape(1, D), swap,
        feats, w_hidden, xi, code, onehot, acc,
    )
    grad, gradt, force_in, pre_grad, heat = outer[:5]
    total = outer[5]
    for got in returned(outer[6:], "gy"):
        total = total + got.astype(F32)
    sends = [total[ux * nzu : (ux + 1) * nzu].astype(BF16) for ux in range(nxu - 1)]
    from_far = swapped(sends, "gx")
    rest = call(
        rest_kernel,
        [((nzu, ROWS, SLOTS), F32)] + [((nzu, ROWS, SLOTS), BF16)] * (nyu - 1),
        table_scratch()
        + buffers
        + [pltpu.VMEM((3,) + square, F32)]
        + sums_scratch(near_cells),
        12,
        [SMEM],
        pair_list, xi, xj, *saved, grad, gradt, force_in,
    )
    energy, direct = call(
        direct_kernel,
        [((1, 1, 1, SLOTS), F32), ((SLOTS, D), F32)],
        [],
        4,
        [],
        pre_grad, heat, w_hidden,
    )
    total = rest[0]
    for got in returned(rest[1:], "gy"):
        total = total + got.astype(F32)
    for got in from_far:
        total = total + got.astype(F32)
    sends = [total[uz : uz + 1].astype(BF16) for uz in range(1, nzu)]
    keep = total[:1]
    arrived = returned(sends, "gz")
    forces, feat_grad = pl.pallas_call(
        lambda *refs: finish_kernel(len(arrived), *refs),
        out_shape=[
            jax.ShapeDtypeStruct((1, 1, 3, 1, SLOTS), F32),
            jax.ShapeDtypeStruct((1, 1, 1, SLOTS, D), BF16),
        ],
        in_specs=[VMEM] * (3 + len(arrived)),
        out_specs=[VMEM] * 2,
        compiler_params=SMALL,
        name="finish",
    )(keep, *arrived, direct, w_env.T)
    return energy, forces.transpose(0, 1, 3, 2, 4), feat_grad


def solution(mesh):
    cell = P("gx", "gy", "gz")
    in_specs = (cell,) * 5 + (P(),) * 7
    return jax.shard_map(
        layer, mesh=mesh, in_specs=in_specs, out_specs=(cell,) * 3, check_vma=False
    )
```
